32 devices in a mesh: groups: 2 (over x), expert: 16 (over z, y, core).
Axes of the slice: x: 2, y: 2, z: 4, core: 2. Of those that a mesh axis runs over, the one named last changes fastest.
Arguments:
- residual: bfloat16 [4096, 3584], P(('groups', 'expert')), parts along dimension 0, may hold values from -24 to 24
- norm_gain: float32 [3584], replicated, may hold values from 0.25 to 1.75
- router: bfloat16 [3584, 4], replicated, may hold values from -0.09375 to 0.09375
- w_gate: bfloat16 [3584, 4096], P(None, 'expert'), may hold values from -0.09375 to 0.09375
- w_up: bfloat16 [3584, 4096], P(None, 'expert'), may hold values from -0.09375 to 0.09375
- w_down: bfloat16 [4096, 3584], P('expert'), may hold values from -0.1875 to 0.1875
- expert_ids: int32 [4096, 2], P(('groups', 'expert')), parts along dimension 0, may hold values from 0 to 3, all different within a row; in each aligned block of 128 rows (0 to 127, 128 to 255, ...) at most 96 rows name the same one
Outputs:
- layer_out: bfloat16 [4096, 3584], P(('groups', 'expert')), parts along dimension 0
The draws below stay inside these ranges and needn't reach their ends.
There are 2 independent parts, one for each index of `groups`. The reference program is written for one: setup_inputs(seed, part) draws one part's arguments, and reference() takes and returns one part's arrays. A program takes and returns all parts, laid end to end along the dimension named above; an argument that names none is the same for every part. Nothing has to cross between parts.
Inputs may be any that keep to these rules, and one draw needn't show every extreme that they name: `expert_ids`: each row names 2 different experts. Within the rows of one device no expert is named by more than 96 rows, and in every draw some device's rows name some expert exactly 96 times.
All inputs are finite; a program needn't handle non-finite values.
Results may differ from the reference program's by a relative error of at most 0.0054.
Values may be sent and summed in bfloat16 or wider, within the bound.
A program may use at most 128 MiB of HBM per device.

```python
import math
import jax
import jax.numpy as jnp
import numpy as np
from jax import lax

D = 3584
FF_E = 1024
SPAN = 4
TOP = 2
TOK_DEV = 128
HID = 256
EXPERTS = 4
TOKENS = 2048
CAP = 96
N_EXPERT = 16


def draw_residual(key, part):
    noise_key = jax.random.fold_in(key, 11)
    column_key = jax.random.fold_in(key, 12)
    row_key = jax.random.fold_in(key, 13)
    column_scale = jnp.exp(jax.random.uniform(column_key, (1, D), jnp.float32, math.log(0.3), math.log(3.0)))
    row_scale = jnp.exp(jax.random.uniform(row_key, (TOKENS, 1), jnp.float32, math.log(0.5), math.log(2.0)))
    base_values = jnp.clip(jax.random.normal(noise_key, (TOKENS, D), jnp.float32), -4.0, 4.0)
    return (base_values * column_scale * row_scale).astype(jnp.bfloat16)


def shard_levels(stream_key, extent, cuts, low, top_value):
    gain, own = 1.0, jax.random.fold_in(stream_key, 6)
    for axis_at, blocks in cuts:
        steps = jnp.exp(jax.random.uniform(jax.random.fold_in(own, axis_at), (blocks,), jnp.float32, low / len(cuts), top_value / len(cuts)))
        gain = gain * jnp.repeat(steps, extent[axis_at] // blocks).reshape([-1 if axis == axis_at else 1 for axis in range(len(extent))])
    return gain


def deal_out(rng, own, number, rows, amount, top, most, skew):
    sequence = jax.random.permutation(rng, amount)
    packed, usual = shares(amount, rows * top, most, skew, True), shares(amount, rows * top, most, skew, False)
    places = jnp.arange(amount)

    def named(tallies, rotation):
        used = int((tallies > 0).sum())
        fixed = max(1, used // 4)
        shifted = fixed + (places - fixed + rotation * (used - fixed)) % max(1, amount - fixed)
        return jnp.zeros((amount,), jnp.int32).at[sequence[jnp.where(places < fixed, places, shifted)]].set(jnp.asarray(tallies, jnp.int32))

    tallies = jnp.where(number % 4 == 0, named(packed, number // 4), named(usual, number - number // 4 - 1))
    mixed = jax.random.permutation(jax.random.fold_in(own, 3), amount)
    giver, receiver = mixed[0:amount // 2 * 2:2], mixed[1:amount // 2 * 2:2]
    margin = jnp.minimum(tallies[giver] - 1, most - tallies[receiver]) // 2
    margin = jnp.where((giver == sequence[0]) | (receiver == sequence[0]) | (tallies[receiver] == 0), 0, jnp.maximum(margin, 0))
    shifted = jax.random.randint(jax.random.fold_in(own, 4), (amount // 2,), 0, 1 << 20) % (margin + 1)
    tallies = tallies.at[giver].add(-shifted).at[receiver].add(shifted)
    items = jnp.searchsorted(jnp.cumsum(tallies), jnp.arange(rows * top), side="right").astype(jnp.int32)
    table = items.reshape(top, rows).T
    table = table[jax.random.permutation(jax.random.fold_in(own, 1), rows)]
    rotation = jax.random.randint(jax.random.fold_in(own, 2), (rows, 1), 0, top)
    return jnp.take_along_axis(table, (jnp.arange(top)[None, :] + rotation) % top, axis=1)


def shares(count, total, reach, slope, full):
    portions = [(1 << 20) // math.isqrt(rank ** slope) + 1 for rank in range(1, count + 1)]
    largest = reach if full else min(reach, max(-(-total // count), total * portions[0] // sum(portions)))
    least = 1 if total - largest >= count - 1 else 0
    counts, spare = [largest] + [least] * (count - 1), total - largest - least * (count - 1)
    while spare > 0:
        free = [i for i in range(1, count) if counts[i] < largest] or [i for i in range(1, count) if counts[i] < reach]
        mass, remaining = sum([portions[i] for i in free]), spare
        for i in free:
            addition = min(reach - counts[i], max(1, remaining * portions[i] // mass), spare)
            counts[i] = counts[i] + addition
            spare = spare - addition
    return np.array(counts)


def scatter_about(stream_key, dims, spread, most, cuts=(), held_as=jnp.bfloat16):
    result = spread * jax.random.normal(stream_key, dims, jnp.float32)
    if cuts:
        result = result * shard_levels(stream_key, dims, cuts, -0.22, 0.18)
    return jnp.clip(result, -most, most).astype(held_as)


def setup_inputs(seed: int = 0, part: int = 0) -> dict:
    keys = jax.random.split(jax.random.key(seed), 8)
    own_keys = jax.random.split(jax.random.fold_in(keys[7], part), 8)
    residual = draw_residual(jax.random.fold_in(jax.random.fold_in(keys[7], part), 71), part)
    norm_gain = jnp.clip(1.0 + 0.15 * jax.random.normal(keys[1], (D,), jnp.float32), 0.25, 1.75)
    router = scatter_about(keys[2], (D, EXPERTS), D ** -0.5, 0.09375)
    w_gate = scatter_about(keys[3], (D, EXPERTS * FF_E), D ** -0.5, 0.09375, ((1, 16),))
    w_up = scatter_about(keys[4], (D, EXPERTS * FF_E), D ** -0.5, 0.09375, ((1, 16),))
    w_down = scatter_about(keys[5], (EXPERTS * FF_E, D), FF_E ** -0.5, 0.1875, ((0, 16),))
    expert_ids_keys = jax.random.split(jax.random.fold_in(own_keys[6], 1), TOKENS // TOK_DEV)
    expert_ids_turns = jax.random.permutation(jax.random.fold_in(own_keys[6], 3), TOKENS // TOK_DEV)
    expert_ids = jax.vmap(lambda own, number: deal_out(jax.random.fold_in(own_keys[6], 2), own, number, TOK_DEV, EXPERTS, TOP, CAP, 2))(expert_ids_keys, expert_ids_turns).reshape((TOKENS, TOP))
    return dict(residual=residual, norm_gain=norm_gain, router=router, w_gate=w_gate, w_up=w_up, w_down=w_down, expert_ids=expert_ids)


route_scale = 2.5
norm_eps = 1e-06

def normalize(residual, norm_gain):
    residual_wide = residual.astype(jnp.float32)
    mean_square = lax.optimization_barrier(jnp.mean(residual_wide * residual_wide, axis=1, keepdims=True))
    normed = (residual_wide * lax.rsqrt(mean_square + norm_eps) * norm_gain).astype(jnp.bfloat16)
    return (residual_wide, normed)

def routing(normed, router, expert_ids):
    logits = jnp.dot(normed, router, preferred_element_type=jnp.float32)
    affinity = jax.nn.sigmoid(logits)
    picked = expert_ids[:, :, None] == lax.iota(jnp.int32, router.shape[1])[None, None, :]
    chosen = lax.optimization_barrier(jnp.sum(jnp.where(picked, affinity[:, None, :], 0.0), axis=2))
    gate_values = route_scale * chosen / lax.optimization_barrier(jnp.sum(chosen, axis=1, keepdims=True))
    return (picked, gate_values)

def slot_numbers(picked, block_rows):
    total_rows, top_count, expert_count = picked.shape
    flat_pick = picked.reshape(total_rows // block_rows, block_rows * top_count, expert_count).astype(jnp.int32)
    before = jnp.cumsum(flat_pick, axis=1) - flat_pick
    return lax.optimization_barrier(jnp.sum(before * flat_pick, axis=2)).reshape(total_rows, top_count)

def reference(residual, norm_gain, router, w_gate, w_up, w_down, expert_ids):
    residual_wide, normed = normalize(residual, norm_gain)
    picked, gate_values = routing(normed, router, expert_ids)
    slot_index = slot_numbers(picked, TOK_DEV)
    block_index = lax.iota(jnp.int32, TOKENS) // TOK_DEV
    position = (block_index[:, None] * CAP + slot_index).astype(jnp.int32)
    owner_row = jnp.broadcast_to(lax.iota(jnp.int32, TOKENS)[:, None], (TOKENS, TOP))
    row_table = jnp.zeros((EXPERTS, N_EXPERT * CAP), jnp.int32).at[expert_ids, position].set(owner_row)
    filled = jnp.zeros((EXPERTS, N_EXPERT * CAP), jnp.int32).at[expert_ids, position].set(1)

    def one_expert(accumulated, expert):
        routed_rows = jnp.take(normed, row_table[expert], axis=0)
        routed_rows = jnp.where(filled[expert][:, None] > 0, routed_rows, jnp.zeros_like(routed_rows))
        summed = jnp.zeros((N_EXPERT * CAP, D), jnp.float32)
        for member in range(SPAN):
            column_start = (expert * SPAN + member) * HID
            gate_proj = jnp.dot(routed_rows, lax.dynamic_slice_in_dim(w_gate, column_start, HID, 1), preferred_element_type=jnp.float32)
            up_proj = jnp.dot(routed_rows, lax.dynamic_slice_in_dim(w_up, column_start, HID, 1), preferred_element_type=jnp.float32)
            activated = (jax.nn.silu(gate_proj) * up_proj).astype(jnp.bfloat16)
            partial_value = jnp.dot(activated, lax.dynamic_slice_in_dim(w_down, column_start, HID, 0), preferred_element_type=jnp.float32).astype(jnp.bfloat16)
            partial_value = lax.optimization_barrier(partial_value)
            summed = summed + partial_value.astype(jnp.float32)
        for route_rank in range(TOP):
            weight = jnp.where(expert_ids[:, route_rank] == expert, gate_values[:, route_rank], 0.0)
            accumulated = accumulated + weight[:, None] * jnp.take(summed, position[:, route_rank], axis=0)
        return (accumulated, None)
    accumulated, unused = lax.scan(one_expert, jnp.zeros((TOKENS, D), jnp.float32), lax.iota(jnp.int32, EXPERTS))
    return (residual_wide + accumulated).astype(jnp.bfloat16)
```

```python
import functools

import jax
import jax.numpy as jnp
from jax import lax
from jax.experimental import pallas as pl
from jax.experimental.pallas import tpu as pltpu
from jax.sharding import PartitionSpec as P

route_scale = 2.5
norm_eps = 1e-06
LANES = 128
MESH = pl.DeviceIdType.MESH

TOK_PIECES = 8
HEAD = 2
OUT_PIECES = 14
W_PIECES = 8
LAG = 2
SHIFT = 1
AHEAD = 2
OWN_TICK = 4


def kernel(
    groups,
    experts,
    span,
    capacity,
    out_pieces,
    res_ref,
    gain_ref,
    router_ref,
    ids_ref,
    wg_in,
    wu_in,
    wd_in,
    out_ref,
    tok,
    gates,
    act,
    rx,
    acc,
    picked,
    wg,
    wu,
    wd,
    own_sem,
    tok_recv,
    tok_send,
    gate_recv,
    gate_send,
    ret_send,
    ret_recv,
    y_send,
    y_recv,
    x_send,
    x_recv,
    c_send,
    c_recv,
    cy_send,
    cy_recv,
    cx_send,
    cx_recv,
):
    rows, width = res_ref.shape
    grp = lax.axis_index("groups")
    pos = lax.axis_index("expert")
    exp = pos // span
    mem = pos % span
    last = experts - 1
    has_up = exp < last
    has_dn = exp > 0
    base = exp * span
    mem_y = (mem + 2) % 4
    mem_c = mem + 1 - 2 * (mem % 2)
    mem_yc = (mem_c + 2) % 4
    up = {"groups": grp, "expert": jnp.minimum(pos + span, experts * span - 1)}
    dn = {"groups": grp, "expert": jnp.maximum(pos - span, 0)}
    to_y = {"groups": grp, "expert": base + mem_y}
    to_c = {"groups": grp, "expert": base + mem_c}

    def other(i):
        return (grp + 1 + i) % groups

    barrier = pltpu.get_barrier_semaphore()

    def greet(device):
        pl.semaphore_signal(barrier, inc=1, device_id=device, device_id_type=MESH)

    greet(to_y)
    greet(to_c)
    for i in range(groups - 1):
        greet({"groups": other(i), "expert": pos})

    @pl.when(has_up)
    def _():
        greet(up)

    @pl.when(has_dn)
    def _():
        greet(dn)

    peers = 1 + groups + has_up.astype(jnp.int32) + has_dn.astype(jnp.int32)
    pl.semaphore_wait(barrier, peers)

    mats = ((wg_in, wg), (wu_in, wu), (wd_in, wd))
    counts = (W_PIECES, W_PIECES, out_pieces)

    def piece(ref, mat, group, index):
        total = mats[mat][0].shape[mat // 2]
        size = total // groups // counts[mat]
        part = pl.ds(pl.multiple_of((index * groups + group) * size, size), size)
        return ref.at[:, part] if mat == 2 else ref.at[part]

    def number(mat, index):
        return sum(counts[:mat]) + index

    def remote(src, dst, send, recv, device):
        return pltpu.make_async_remote_copy(
            src_ref=src, dst_ref=dst, send_sem=send, recv_sem=recv, device_id=device, device_id_type=MESH
        )

    def y_copy(mat, index, landing):
        at = number(mat, index)
        into = piece(mats[mat][1].at[mem_y if landing else mem], mat, grp, index)
        return remote(piece(mats[mat][0], mat, grp, index), into, y_send.at[at], y_recv.at[at], to_y)

    def x_copy(mat, index, i, landing):
        at = number(mat, index)
        group = (grp + groups - 1 - i) % groups if landing else grp
        ref = piece(mats[mat][1].at[mem_y], mat, group, index)
        return remote(ref, ref, x_send.at[i, at], x_recv.at[i, at], {"groups": other(i), "expert": pos})

    def cy_copy(mat, index, landing):
        at = number(mat, index)
        ref = piece(mats[mat][1].at[mem_yc if landing else mem_y], mat, grp, index)
        return remote(ref, ref, cy_send.at[at], cy_recv.at[at], to_c)

    def cx_copy(mat, index, i, landing):
        at = number(mat, index)
        group = (grp + groups - 1 - i) % groups
        ref = piece(mats[mat][1].at[mem_yc if landing else mem_y], mat, group, index)
        return remote(ref, ref, cx_send.at[i, at], cx_recv.at[i, at], to_c)

    def c_copy(mat, landing):
        slot = mem_c if landing else mem
        return remote(mats[mat][0], mats[mat][1].at[slot], c_send.at[mat], c_recv.at[mat], to_c)

    def loop(count, body):
        def run(i, carry):
            body(i)
            return carry

        lax.fori_loop(0, count, run, 0)

    def start_pair(index):
        for mat in range(2):
            y_copy(mat, index, False).start()

    loop(W_PIECES, start_pair)
    loop(out_pieces, lambda index: y_copy(2, index, False).start())
    own_copies = [pltpu.make_async_copy(mats[i][0], mats[i][1].at[mem], own_sem.at[i]) for i in range(3)]
    for mat in range(3):
        c_copy(mat, False).start()
        own_copies[mat].start()

    step_rows = rows // TOK_PIECES
    tail = TOK_PIECES - HEAD
    ticks = (experts - 2) * TOK_PIECES
    behind = (exp, last - exp)
    onward = (has_up, has_dn)

    def tok_copy(block, index, way):
        ref = tok.at[block, pl.ds(pl.multiple_of(index * step_rows, step_rows), step_rows)]
        return remote(ref, ref, tok_send.at[way, block, index], tok_recv.at[block, index], (up, dn)[way])

    def gate_copy(block, way):
        ref = gates.at[block]
        return remote(ref, ref, gate_send.at[way, block], gate_recv.at[block], (up, dn)[way])

    def norm_rows(index):
        at = pl.ds(pl.multiple_of(index * step_rows, step_rows), step_rows)
        wide = res_ref[at, :].astype(jnp.float32)
        mean = jnp.mean(wide * wide, axis=1, keepdims=True)
        tok[exp, at, :] = (wide * lax.rsqrt(mean + norm_eps) * gain_ref[...].reshape(1, width)).astype(jnp.bfloat16)
        for way in range(2):
            early = jnp.logical_or(index < HEAD, behind[way] == 0)

            @pl.when(jnp.logical_and(onward[way], early))
            def _():
                tok_copy(exp, index, way).start()

    def gate_values():
        logits = lax.dot_general(
            router_ref[...], tok[exp], (((1,), (1,)), ((), ())), preferred_element_type=jnp.float32
        )
        affinity = jax.nn.sigmoid(logits)
        expert = lax.broadcasted_iota(jnp.int32, (experts, rows), 0)
        spread = jnp.zeros((experts, rows), jnp.float32)
        for k in range(ids_ref.shape[0]):
            spread = spread + jnp.where(expert == ids_ref[k : k + 1, :], affinity, 0.0)
        gates[exp] = route_scale * spread / jnp.sum(spread, axis=0, keepdims=True)

    loop(TOK_PIECES, norm_rows)
    gate_values()
    for way in range(2):

        @pl.when(jnp.logical_and(onward[way], behind[way] == 0))
        def _():
            gate_copy(exp, way).start()

    def weight_tick(mat, index):
        y_copy(mat, index, True).wait_recv()
        for i in range(groups - 1):
            x_copy(mat, index, i, False).start()
        cy_copy(mat, index, False).start()

    def weight_late(mat, index):
        for i in range(groups - 1):
            x_copy(mat, index, i, True).wait_recv()
            cx_copy(mat, index, i, False).start()

    def weight_there(mat, index):
        cy_copy(mat, index, True).wait_recv()
        for i in range(groups - 1):
            cx_copy(mat, index, i, True).wait_recv()

    def token_tick(tick, way):
        count = behind[way]
        rest = jnp.maximum(tick - count * HEAD, 0)
        leading = tick < count * HEAD
        dist = jnp.where(leading, tick // HEAD + 1, count - rest // tail)
        dist = jnp.maximum(dist, 1)
        index = jnp.where(leading, tick % HEAD, HEAD + rest % tail)
        block = jnp.maximum(exp - dist, 0) if way == 0 else jnp.minimum(exp + dist, last)
        whole = index == TOK_PIECES - 1

        @pl.when(tick < count * TOK_PIECES)
        def _():
            tok_copy(block, index, way).wait_recv()

            @pl.when(whole)
            def _():
                gate_copy(block, way).wait_recv()

            @pl.when(onward[way])
            def _():
                tok_copy(block, index, way).start()

                @pl.when(whole)
                def _():
                    gate_copy(block, way).start()

                @pl.when(tick == count * TOK_PIECES - 1)
                def _():
                    for own in range(HEAD, TOK_PIECES):
                        tok_copy(exp, own, way).start()
                    gate_copy(exp, way).start()

    def hidden_part(block, slot):
        rows_in = tok[block]
        gate_proj = jnp.dot(rows_in, wg[slot], preferred_element_type=jnp.float32)
        up_proj = jnp.dot(rows_in, wu[slot], preferred_element_type=jnp.float32)
        sublane = lax.broadcasted_iota(jnp.int32, (gates.shape[1], rows), 0)
        row = jnp.sum(jnp.where(sublane == exp, gates[block], 0.0), axis=0, keepdims=True)
        scale = jnp.broadcast_to(row, (LANES, rows)).T[:, :1]
        hidden = gate_proj / (1.0 + jnp.exp(-gate_proj)) * up_proj * scale
        act[slot, block] = hidden.astype(jnp.bfloat16)

    def whole_at(way, dist):
        count = behind[way]
        return count * HEAD + (count - dist + 1) * tail

    def found(tick, way):
        count = behind[way]
        over = tick + 1 - count * HEAD
        dist = count + 1 - over // tail
        there = jnp.logical_and(over > 0, over % tail == 0)
        return jnp.logical_and(there, jnp.logical_and(dist >= 1, dist <= count)), dist

    def first_tick(tick):
        for mat in range(2):

            @pl.when(jnp.logical_and(tick < 2 * W_PIECES, tick % 2 == mat))
            def _():
                weight_tick(mat, tick // 2)

        token_tick(tick, 0)
        token_tick(tick, 1)
        for mat in range(2):
            before = tick - 1

            @pl.when(jnp.logical_and(jnp.logical_and(before >= 0, before < 2 * W_PIECES), tick % 2 != mat))
            def _():
                weight_late(mat, jnp.maximum(before, 0) // 2)

        @pl.when(tick == OWN_TICK)
        def _():
            for mat in range(2):
                own_copies[mat].wait()
                c_copy(mat, True).wait_recv()

        from_dn, dist_dn = found(tick, 0)
        from_up, dist_up = found(tick, 1)
        own = tick == OWN_TICK

        def job(i):
            side = i // 2
            slot = jnp.where(i % 2 == 0, mem, mem_c)
            block = jnp.where(side == 0, exp - dist_dn, jnp.where(side == 1, exp + dist_up, exp))
            valid = jnp.logical_or(
                jnp.logical_and(side == 0, from_dn),
                jnp.logical_or(jnp.logical_and(side == 1, from_up), jnp.logical_and(side == 2, own)),
            )

            @pl.when(valid)
            def _():
                hidden_part(jnp.clip(block, 0, last), slot)

        @pl.when(jnp.logical_or(own, jnp.logical_or(from_dn, from_up)))
        def _():
            loop(6, job)

    total = max(ticks, 2 * W_PIECES, OWN_TICK + 1)
    loop(total, first_tick)
    for index in range(AHEAD):
        weight_tick(2, index)
    if total == 2 * W_PIECES:
        weight_late(1, W_PIECES - 1)
    for index in range(AHEAD - 1):
        weight_late(2, index)

    def pair_there(index):
        for mat in range(2):
            weight_there(mat, index)

    loop(W_PIECES, pair_there)

    def far_job(i):
        dist = last - i // 4
        side = i // 2 % 2
        slot = jnp.where(i % 2 == 0, mem_y, mem_yc)
        valid = False
        for way in range(2):
            full = jnp.logical_and(dist <= behind[way], whole_at(way, dist) <= ticks)
            valid = jnp.logical_or(valid, jnp.logical_and(side == way, full))
        block = jnp.where(side == 0, exp - dist, exp + dist)

        @pl.when(valid)
        def _():
            hidden_part(jnp.clip(block, 0, last), slot)

    loop(4 * last, far_job)
    own_copies[2].wait()
    c_copy(2, True).wait_recv()

    cols = width // out_pieces

    def columns(index):
        return pl.ds(pl.multiple_of(index * cols, cols), cols)

    def out_copy(block, index, way, landing, packed):
        part = columns(index)
        height = pl.ds(0, capacity if packed else rows)
        target = exp if landing else exp - 1
        into = jnp.where(jnp.logical_and(way == 1, block == target), experts, block)
        along = jnp.where(way == 0, jnp.minimum(pos + span, experts * span - 1), jnp.maximum(pos - span, 0))
        return remote(
            tok.at[block, height, part],
            rx.at[into, height, part],
            ret_send.at[block, index],
            ret_recv.at[into, index],
            {"groups": grp, "expert": along},
        )

    def share(block, at, height=rows):
        part = pl.ds(0, height)
        result = jnp.dot(act[0, block, part], wd[0, :, at], preferred_element_type=jnp.float32)
        for slot in range(1, span):
            result = result + jnp.dot(act[slot, block, part], wd[slot, :, at], preferred_element_type=jnp.float32)
        return result

    def packing(block, expert):
        sublane = lax.broadcasted_iota(jnp.int32, (gates.shape[1], rows), 0)
        row = jnp.sum(jnp.where(sublane == expert, gates[block], 0.0), axis=0, keepdims=True)
        taken = jnp.broadcast_to(jnp.where(row != 0.0, 1.0, 0.0), (capacity, rows))
        source = lax.broadcasted_iota(jnp.int32, (rows, rows), 0)
        dest = lax.broadcasted_iota(jnp.int32, (rows, rows), 1)
        earlier = jnp.where(source < dest, 1.0, 0.0).astype(jnp.bfloat16)
        rank = jnp.dot(taken.astype(jnp.bfloat16), earlier, preferred_element_type=jnp.float32)
        slot = lax.broadcasted_iota(jnp.int32, (capacity, rows), 0).astype(jnp.float32)
        return jnp.where(rank == slot, taken, 0.0).astype(jnp.bfloat16)

    def unpacked(way, block, value):
        return lax.dot_general(
            picked[way, block], value, (((0,), (0,)), ((), ())), preferred_element_type=jnp.float32
        )

    def late_rows(block, dist, way):
        for index in range(HEAD, TOK_PIECES):

            @pl.when(jnp.logical_or(dist == 1, index >= TOK_PIECES - HEAD))
            def _():
                tok_copy(block, index, 0).wait_recv()

        gate_copy(block, 0).wait_recv()
        loop(span, lambda slot: hidden_part(block, slot))

    def send_result(block, index, way, dist, count):
        at = columns(index)

        @pl.when(count == 0)
        def _():
            @pl.when(jnp.logical_and(dist <= 2, index == 0))
            def _():
                late_rows(block, dist, way)

            @pl.when(index == 0)
            def _():
                picks = packing(block, exp)

                def pack(slot):
                    act[slot, block, pl.ds(0, capacity)] = jnp.dot(
                        picks, act[slot, block], preferred_element_type=jnp.float32
                    ).astype(jnp.bfloat16)

                loop(span, pack)

            tok[block, pl.ds(0, capacity), at] = share(block, at, capacity).astype(jnp.bfloat16)
            out_copy(block, index, way, False, True).start()

        @pl.when(jnp.logical_and(count > 0, index == 0))
        def _():
            for i in range(TOK_PIECES):
                tok_copy_way(block, i, 1 - way).wait_send()
            gate_copy_way(block, 1 - way).wait_send()

        @pl.when(count == 1)
        def _():
            @pl.when(index == 0)
            def _():
                picked[way, block] = packing(block, jnp.where(way == 0, exp - 1, exp + 1))

            out_copy(block, index, way, True, True).wait_recv()
            result = share(block, at) + unpacked(way, block, rx[block, pl.ds(0, capacity), at])
            tok[block, :, at] = result.astype(jnp.bfloat16)

        @pl.when(count > 1)
        def _():
            out_copy(block, index, way, True, False).wait_recv()
            result = share(block, at) + rx[block, :, at].astype(jnp.float32)
            tok[block, :, at] = result.astype(jnp.bfloat16)

        @pl.when(count > 0)
        def _():
            out_copy(block, index, way, False, False).start()

    def tok_copy_way(block, index, way):
        ref = tok.at[block, pl.ds(pl.multiple_of(index * step_rows, step_rows), step_rows)]
        along = jnp.where(way == 0, up["expert"], dn["expert"])
        device = {"groups": grp, "expert": along}
        return remote(ref, ref, tok_send.at[way, block, index], tok_recv.at[block, index], device)

    def gate_copy_way(block, way):
        ref = gates.at[block]
        along = jnp.where(way == 0, up["expert"], dn["expert"])
        device = {"groups": grp, "expert": along}
        return remote(ref, ref, gate_send.at[way, block], gate_recv.at[block], device)

    def join(index, way, count):
        at = columns(index)
        slot = jnp.where(way == 0, exp, experts)

        @pl.when(count == 1)
        def _():
            @pl.when(index == 0)
            def _():
                picked[way, exp] = packing(exp, jnp.where(way == 0, exp - 1, exp + 1))

            out_copy(exp, index, way, True, True).wait_recv()
            acc[:, at] += unpacked(way, exp, rx[slot, pl.ds(0, capacity), at])

        @pl.when(count > 1)
        def _():
            out_copy(exp, index, way, True, False).wait_recv()
            acc[:, at] += rx[slot, :, at].astype(jnp.float32)

        out_ref[:, at] = acc[:, at].astype(jnp.bfloat16)

    period = out_pieces + SHIFT

    def role(tick, i):
        way = i % 2
        second = i // 2
        count = jnp.where(way == 0, exp, last - exp)
        ahead = last - count
        time = tick - LAG * count
        clock = jnp.maximum(time, 0)
        pair = clock // period
        index = clock % period - SHIFT * second
        far = 2 * pair + second
        dist = ahead - far
        block = jnp.clip(jnp.where(way == 0, exp + dist, exp - dist), 0, last)
        there = jnp.logical_and(time >= 0, jnp.logical_and(index >= 0, index < out_pieces))
        index = jnp.clip(index, 0, out_pieces - 1)

        @pl.when(jnp.logical_and(there, dist > 0))
        def _():
            send_result(block, index, way, dist, count)

        @pl.when(jnp.logical_and(there, jnp.logical_and(dist == 0, count > 0)))
        def _():
            join(index, way, count)

    def second_tick(tick):
        @pl.when(tick + AHEAD < out_pieces)
        def _():
            weight_tick(2, jnp.minimum(tick + AHEAD, out_pieces - 1))

        @pl.when(tick + AHEAD - 1 < out_pieces)
        def _():
            weight_late(2, jnp.minimum(tick + AHEAD - 1, out_pieces - 1))

        @pl.when(tick < out_pieces)
        def _():
            weight_there(2, jnp.minimum(tick, out_pieces - 1))

        loop(4, lambda i: role(tick, i))

        @pl.when(tick == 1)
        def _():
            loop(2, lambda i: hidden_part(exp, jnp.where(i == 0, mem_y, mem_yc)))

        @pl.when(jnp.logical_and(tick >= 1, tick < out_pieces + 1))
        def _():
            at = columns(jnp.clip(tick - 1, 0, out_pieces - 1))
            acc[:, at] = res_ref[:, at].astype(jnp.float32) + share(exp, at)

    loop(-(-experts // 2) * period + LAG * last, second_tick)

    def own_sent(way):
        @pl.when(onward[way])
        def _():
            for index in range(TOK_PIECES):
                tok_copy(exp, index, way).wait_send()
            gate_copy(exp, way).wait_send()

    own_sent(0)
    own_sent(1)

    def results_sent(block):
        def drain(way, packed):
            loop(out_pieces, lambda index: out_copy(block, index, way, False, packed).wait_send())

        for way in range(2):
            passes = block > exp if way == 0 else block < exp

            @pl.when(jnp.logical_and(passes, behind[way] == 0))
            def _():
                drain(way, True)

            @pl.when(jnp.logical_and(passes, behind[way] > 0))
            def _():
                drain(way, False)

    loop(experts, results_sent)

    def weights_sent(mat, index):
        y_copy(mat, index, False).wait_send()
        cy_copy(mat, index, False).wait_send()
        for i in range(groups - 1):
            x_copy(mat, index, i, False).wait_send()
            cx_copy(mat, index, i, False).wait_send()

    for mat in range(3):
        c_copy(mat, False).wait_send()
        loop(counts[mat], functools.partial(weights_sent, mat))


def shards(residual, norm_gain, router, w_gate, w_up, w_down, expert_ids):
    rows, width = residual.shape
    experts = router.shape[1]
    groups = lax.axis_size("groups")
    span = lax.axis_size("expert") // experts
    assert span == 4
    hid = w_gate.shape[1]
    capacity = 3 * rows * expert_ids.shape[1] // (2 * experts)
    capacity = min(rows, -(-capacity // 16) * 16)
    out_pieces = min(OUT_PIECES, width // (groups * LANES))
    vmem = pl.BlockSpec(memory_space=pltpu.VMEM)
    anywhere = pl.BlockSpec(memory_space=pl.ANY)
    dma = pltpu.SemaphoreType.DMA
    weight_copies = 2 * W_PIECES + out_pieces
    return pl.pallas_call(
        functools.partial(kernel, groups, experts, span, capacity, out_pieces),
        out_shape=jax.ShapeDtypeStruct((rows, width), jnp.bfloat16),
        in_specs=[vmem, vmem, vmem, vmem, anywhere, anywhere, anywhere],
        out_specs=vmem,
        scratch_shapes=[
            pltpu.VMEM((experts, rows, width), jnp.bfloat16),
            pltpu.VMEM((experts, experts, rows), jnp.float32),
            pltpu.VMEM((span, experts, rows, hid), jnp.bfloat16),
            pltpu.VMEM((experts + 1, rows, width), jnp.bfloat16),
            pltpu.VMEM((rows, width), jnp.float32),
            pltpu.VMEM((2, experts, capacity, rows), jnp.bfloat16),
            pltpu.VMEM((span, width, hid), jnp.bfloat16),
            pltpu.VMEM((span, width, hid), jnp.bfloat16),
            pltpu.VMEM((span, hid, width), jnp.bfloat16),
            dma((3,)),
            dma((experts, TOK_PIECES)),
            dma((2, experts, TOK_PIECES)),
            dma((experts,)),
            dma((2, experts)),
            dma((experts, out_pieces)),
            dma((experts + 1, out_pieces)),
            dma((weight_copies,)),
            dma((weight_copies,)),
            dma((groups - 1, weight_copies)),
            dma((groups - 1, weight_copies)),
            dma((3,)),
            dma((3,)),
            dma((weight_copies,)),
            dma((weight_copies,)),
            dma((groups - 1, weight_copies)),
            dma((groups - 1, weight_copies)),
        ],
        compiler_params=pltpu.CompilerParams(
            collective_id=0, has_side_effects=True, vmem_limit_bytes=67043328
        ),
    )(residual, norm_gain, router.T, expert_ids.T, w_gate, w_up, w_down)


def solution(mesh):
    in_specs = (
        P(("groups", "expert"), None),
        P(),
        P(),
        P(None, "expert"),
        P(None, "expert"),
        P("expert", None),
        P(("groups", "expert"), None),
    )
    out_specs = P(("groups", "expert"), None)
    return jax.shard_map(shards, mesh=mesh, in_specs=in_specs, out_specs=out_specs, check_vma=False)
```

```python
import functools

import jax
import jax.numpy as jnp
from jax import lax
from jax.experimental import pallas as pl
from jax.experimental.pallas import tpu as pltpu
from jax.sharding import PartitionSpec as P

route_scale = 2.5
norm_eps = 1e-06
LANES = 128
MESH = pl.DeviceIdType.MESH

TOK_PIECES = 8
HEAD = 2
OUT_PIECES = 14
W_PIECES = 16
LAG = 2
SHIFT = 3
LATE = 2
AHEAD = 3
LATE_DOWN = 1
NEAR = 3
NEAR_TICKS = 4
OWN_TICK = 4


def kernel(
    groups,
    experts,
    span,
    capacity,
    out_pieces,
    w_pieces,
    res_in,
    gain_in,
    router_in,
    ids_in,
    wg_in,
    wu_in,
    wd_in,
    out_ref,
    res_ref,
    gain_ref,
    router_ref,
    ids_ref,
    tok,
    gates,
    act,
    rx,
    acc,
    picked,
    wg,
    wu,
    wd,
    in_sem,
    own_sem,
    tok_recv,
    tok_send,
    gate_recv,
    gate_send,
    ret_send,
    ret_recv,
    y_send,
    y_recv,
    x_send,
    x_recv,
    c_send,
    c_recv,
    cy_send,
    cy_recv,
    cx_send,
    cx_recv,
):
    rows, width = res_ref.shape
    grp = lax.axis_index("groups")
    pos = lax.axis_index("expert")
    exp = pos // span
    mem = pos % span
    last = experts - 1
    has_up = exp < last
    has_dn = exp > 0
    base = exp * span
    mem_y = (mem + 2) % 4
    mem_c = mem + 1 - 2 * (mem % 2)
    mem_yc = (mem_c + 2) % 4
    up = {"groups": grp, "expert": jnp.minimum(pos + span, experts * span - 1)}
    dn = {"groups": grp, "expert": jnp.maximum(pos - span, 0)}
    to_y = {"groups": grp, "expert": base + mem_y}
    to_c = {"groups": grp, "expert": base + mem_c}

    def other(i):
        return (grp + 1 + i) % groups

    barrier = pltpu.get_barrier_semaphore()

    def greet(device):
        pl.semaphore_signal(barrier, inc=1, device_id=device, device_id_type=MESH)

    greet(to_y)
    greet(to_c)
    for i in range(groups - 1):
        greet({"groups": other(i), "expert": pos})

    @pl.when(has_up)
    def _():
        greet(up)

    @pl.when(has_dn)
    def _():
        greet(dn)

    inputs = ((res_in, res_ref), (gain_in, gain_ref), (router_in, router_ref), (ids_in, ids_ref))
    loads = [pltpu.make_async_copy(*pair, in_sem.at[i]) for i, pair in enumerate(inputs)]
    for load in loads:
        load.start()

    mats = ((wg_in, wg), (wu_in, wu), (wd_in, wd))
    counts = (w_pieces, w_pieces, out_pieces)

    def piece(ref, mat, group, index):
        total = mats[mat][0].shape[mat // 2]
        size = total // groups // counts[mat]
        part = pl.ds(pl.multiple_of((index * groups + group) * size, size), size)
        return ref.at[:, part] if mat == 2 else ref.at[part]

    def number(mat, index):
        return sum(counts[:mat]) + index

    def remote(src, dst, send, recv, device):
        return pltpu.make_async_remote_copy(
            src_ref=src, dst_ref=dst, send_sem=send, recv_sem=recv, device_id=device, device_id_type=MESH
        )

    def y_copy(mat, index, landing):
        at = number(mat, index)
        into = piece(mats[mat][1].at[mem_y if landing else mem], mat, grp, index)
        return remote(piece(mats[mat][0], mat, grp, index), into, y_send.at[mat], y_recv.at[at], to_y)

    def x_copy(mat, index, i, landing):
        at = number(mat, index)
        group = (grp + groups - 1 - i) % groups if landing else grp
        ref = piece(mats[mat][1].at[mem_y], mat, group, index)
        return remote(ref, ref, x_send.at[i, mat], x_recv.at[i, at], {"groups": other(i), "expert": pos})

    def landed(mat, index):
        return mat if mat < 2 else 2 + index

    def cy_copy(mat, index, landing):
        at = landed(mat, index)
        ref = piece(mats[mat][1].at[mem_yc if landing else mem_y], mat, grp, index)
        return remote(ref, ref, cy_send.at[mat], cy_recv.at[at], to_c)

    def cx_copy(mat, index, i, landing):
        at = landed(mat, index)
        group = (grp + groups - 1 - i) % groups
        ref = piece(mats[mat][1].at[mem_yc if landing else mem_y], mat, group, index)
        return remote(ref, ref, cx_send.at[i, mat], cx_recv.at[i, at], to_c)

    def all_pieces(mat, send, recv, device):
        ref = mats[mat][1].at[mem_y]
        part = pl.ds(0, mats[mat][0].shape[mat // 2] // groups)
        ref = ref.at[:, part] if mat == 2 else ref.at[part]
        return remote(ref, ref, send, recv, device)

    def c_copy(mat, landing):
        slot = mem_c if landing else mem
        return remote(mats[mat][0], mats[mat][1].at[slot], c_send.at[mat], c_recv.at[mat], to_c)

    def loop(count, body):
        def run(i, carry):
            body(i)
            return carry

        lax.fori_loop(0, count, run, 0)

    def start_pair(index):
        for mat in range(2):
            y_copy(mat, index, False).start()

    own_copies = [pltpu.make_async_copy(mats[i][0], mats[i][1].at[mem], own_sem.at[i]) for i in range(3)]

    step_rows = rows // TOK_PIECES
    tail = TOK_PIECES - HEAD
    ticks = (experts - 2) * TOK_PIECES
    behind = (exp, last - exp)
    onward = (has_up, has_dn)

    def tok_copy(block, index, way):
        ref = tok.at[block, pl.ds(pl.multiple_of(index * step_rows, step_rows), step_rows)]
        return remote(ref, ref, tok_send.at[way, block], tok_recv.at[block, index], (up, dn)[way])

    def gate_copy(block, way):
        ref = gates.at[block]
        return remote(ref, ref, gate_send.at[way, block], gate_recv.at[block], (up, dn)[way])

    def norm_rows(index):
        at = pl.ds(pl.multiple_of(index * step_rows, step_rows), step_rows)
        wide = res_ref[at, :].astype(jnp.float32)
        mean = jnp.mean(wide * wide, axis=1, keepdims=True)
        tok[exp, at, :] = (wide * lax.rsqrt(mean + norm_eps) * gain_ref[...]).astype(jnp.bfloat16)

    def first_rows(index):
        for way in range(2):
            early = jnp.logical_or(index < HEAD, behind[way] == 0)

            @pl.when(jnp.logical_and(onward[way], early))
            def _():
                tok_copy(exp, index, way).start()

    def gate_values():
        logits = lax.dot_general(
            router_ref[...], tok[exp], (((1,), (1,)), ((), ())), preferred_element_type=jnp.float32
        )
        affinity = jax.nn.sigmoid(logits)
        expert = lax.broadcasted_iota(jnp.int32, (experts, rows), 0)
        spread = jnp.zeros((experts, rows), jnp.float32)
        for k in range(ids_ref.shape[0]):
            spread = spread + jnp.where(expert == ids_ref[k : k + 1, :], affinity, 0.0)
        gates[exp] = route_scale * spread / jnp.sum(spread, axis=0, keepdims=True)

    peers = 1 + groups + has_up.astype(jnp.int32) + has_dn.astype(jnp.int32)
    pl.semaphore_wait(barrier, peers)
    loop(w_pieces, start_pair)
    for load in loads:
        load.wait()

    def first_step(index):
        norm_rows(index)
        first_rows(index)

    loop(TOK_PIECES, first_step)
    loop(out_pieces, lambda index: y_copy(2, index, False).start())
    for mat in range(3):
        c_copy(mat, False).start()
        own_copies[mat].start()
    gate_values()
    for way in range(2):

        @pl.when(jnp.logical_and(onward[way], behind[way] == 0))
        def _():
            gate_copy(exp, way).start()

    def weight_tick(mat, index):
        y_copy(mat, index, True).wait_recv()
        for i in range(groups - 1):
            x_copy(mat, index, i, False).start()
        cy_copy(mat, index, False).start()

    def weight_late(mat, index):
        for i in range(groups - 1):
            x_copy(mat, index, i, True).wait_recv()
            cx_copy(mat, index, i, False).start()

    def down_there(index):
        cy_copy(2, index, True).wait_recv()
        for i in range(groups - 1):
            cx_copy(2, index, i, True).wait_recv()

    def token_tick(tick, way):
        count = behind[way]
        rest = jnp.maximum(tick - count * HEAD, 0)
        leading = tick < count * HEAD
        dist = jnp.where(leading, tick // HEAD + 1, count - rest // tail)
        dist = jnp.maximum(dist, 1)
        index = jnp.where(leading, tick % HEAD, HEAD + rest % tail)
        block = jnp.maximum(exp - dist, 0) if way == 0 else jnp.minimum(exp + dist, last)
        whole = index == TOK_PIECES - 1

        @pl.when(tick < count * TOK_PIECES)
        def _():
            tok_copy(block, index, way).wait_recv()

            @pl.when(whole)
            def _():
                gate_copy(block, way).wait_recv()

            @pl.when(onward[way])
            def _():
                tok_copy(block, index, way).start()

                @pl.when(whole)
                def _():
                    gate_copy(block, way).start()

                @pl.when(tick == count * TOK_PIECES - 1)
                def _():
                    for own in range(HEAD, TOK_PIECES):
                        tok_copy(exp, own, way).start()
                    gate_copy(exp, way).start()

    def hidden_part(block, slot):
        rows_in = tok[block]
        gate_proj = jnp.dot(rows_in, wg[slot], preferred_element_type=jnp.float32)
        up_proj = jnp.dot(rows_in, wu[slot], preferred_element_type=jnp.float32)
        sublane = lax.broadcasted_iota(jnp.int32, (gates.shape[1], rows), 0)
        row = jnp.sum(jnp.where(sublane == exp, gates[block], 0.0), axis=0, keepdims=True)
        scale = jnp.broadcast_to(row, (LANES, rows)).T[:, :1]
        hidden = gate_proj / (1.0 + jnp.exp(-gate_proj)) * up_proj * scale
        act[slot, block] = hidden.astype(jnp.bfloat16)

    def whole_at(way, dist):
        count = behind[way]
        return count * HEAD + (count - dist + 1) * tail

    def found(tick, way):
        count = behind[way]
        over = tick + 1 - count * HEAD
        dist = count + 1 - over // tail
        there = jnp.logical_and(over > 0, over % tail == 0)
        return jnp.logical_and(there, jnp.logical_and(dist >= 1, dist <= count)), dist

    def first_tick(tick):
        @pl.when(tick < w_pieces)
        def _():
            weight_tick(0, tick)

        token_tick(tick, 0)
        token_tick(tick, 1)

        @pl.when(tick < w_pieces)
        def _():
            weight_tick(1, tick)

        before = tick - LATE

        @pl.when(jnp.logical_and(before >= 0, before < w_pieces))
        def _():
            weight_late(0, jnp.maximum(before, 0))
            weight_late(1, jnp.maximum(before, 0))

        @pl.when(tick == OWN_TICK)
        def _():
            for mat in range(2):
                own_copies[mat].wait()
                c_copy(mat, True).wait_recv()

        from_dn, dist_dn = found(tick, 0)
        from_up, dist_up = found(tick, 1)
        own = tick == OWN_TICK

        def job(i):
            side = i // 2
            slot = jnp.where(i % 2 == 0, mem, mem_c)
            block = jnp.where(side == 0, exp - dist_dn, jnp.where(side == 1, exp + dist_up, exp))
            valid = jnp.logical_or(
                jnp.logical_and(side == 0, from_dn),
                jnp.logical_or(jnp.logical_and(side == 1, from_up), jnp.logical_and(side == 2, own)),
            )

            @pl.when(valid)
            def _():
                hidden_part(jnp.clip(block, 0, last), slot)

        @pl.when(jnp.logical_or(own, jnp.logical_or(from_dn, from_up)))
        def _():
            loop(6, job)

    total = max(ticks, w_pieces, OWN_TICK + 1)
    loop(total, first_tick)
    rest = [(mat, before) for before in range(total - LATE, w_pieces) for mat in range(2)]
    for index in range(max(len(rest), AHEAD - 1)):
        if index < len(rest):
            weight_late(*rest[index])
        if index < AHEAD - 1:
            weight_tick(2, index)
    for index in range(LATE_DOWN):
        weight_late(2, index)
    for mat in range(2):
        all_pieces(mat, cy_send.at[mat], cy_recv.at[mat], to_c).wait_recv()
        for i in range(groups - 1):
            all_pieces(mat, cx_send.at[i, mat], cx_recv.at[i, mat], to_c).wait_recv()
    weight_tick(2, AHEAD - 1)

    def far_job(i):
        dist = last - i // 4
        side = i // 2 % 2
        slot = jnp.where(i % 2 == 0, mem_y, mem_yc)
        valid = False
        for way in range(2):
            full = jnp.logical_and(dist <= behind[way], whole_at(way, dist) <= ticks)
            valid = jnp.logical_or(valid, jnp.logical_and(side == way, full))
        block = jnp.where(side == 0, exp - dist, exp + dist)

        @pl.when(valid)
        def _():
            hidden_part(jnp.clip(block, 0, last), slot)

    loop(4 * last, far_job)
    own_copies[2].wait()
    c_copy(2, True).wait_recv()

    cols = width // out_pieces

    def columns(index):
        return pl.ds(pl.multiple_of(index * cols, cols), cols)

    def out_copy(block, index, way, landing, packed):
        part = columns(index)
        height = pl.ds(0, capacity if packed else rows)
        target = exp if landing else exp - 1
        into = jnp.where(jnp.logical_and(way == 1, block == target), experts, block)
        along = jnp.where(way == 0, jnp.minimum(pos + span, experts * span - 1), jnp.maximum(pos - span, 0))
        return remote(
            tok.at[block, height, part],
            rx.at[into, height, part],
            ret_send.at[block],
            ret_recv.at[into, index],
            {"groups": grp, "expert": along},
        )

    def share(block, at, height=rows):
        part = pl.ds(0, height)
        result = jnp.dot(act[0, block, part], wd[0, :, at], preferred_element_type=jnp.float32)
        for slot in range(1, span):
            result = result + jnp.dot(act[slot, block, part], wd[slot, :, at], preferred_element_type=jnp.float32)
        return result

    def packing(block, expert):
        sublane = lax.broadcasted_iota(jnp.int32, (gates.shape[1], rows), 0)
        row = jnp.sum(jnp.where(sublane == expert, gates[block], 0.0), axis=0, keepdims=True)
        taken = jnp.broadcast_to(jnp.where(row != 0.0, 1.0, 0.0), (capacity, rows))
        source = lax.broadcasted_iota(jnp.int32, (rows, rows), 0)
        dest = lax.broadcasted_iota(jnp.int32, (rows, rows), 1)
        earlier = jnp.where(source < dest, 1.0, 0.0).astype(jnp.bfloat16)
        rank = jnp.dot(taken.astype(jnp.bfloat16), earlier, preferred_element_type=jnp.float32)
        slot = lax.broadcasted_iota(jnp.int32, (capacity, rows), 0).astype(jnp.float32)
        return jnp.where(rank == slot, taken, 0.0).astype(jnp.bfloat16)

    def unpacked(way, block, value):
        return lax.dot_general(
            picked[way, block], value, (((0,), (0,)), ((), ())), preferred_element_type=jnp.float32
        )

    def late_rows(block, dist):
        for index in range(HEAD, TOK_PIECES):

            @pl.when(jnp.logical_or(dist == 1, index >= TOK_PIECES - HEAD))
            def _():
                tok_copy(block, index, 0).wait_recv()

        gate_copy(block, 0).wait_recv()

    def send_result(block, index, way, count):
        at = columns(index)

        @pl.when(count == 0)
        def _():
            @pl.when(index == 0)
            def _():
                picks = packing(block, exp)

                def pack(slot):
                    act[slot, block, pl.ds(0, capacity)] = jnp.dot(
                        picks, act[slot, block], preferred_element_type=jnp.float32
                    ).astype(jnp.bfloat16)

                loop(span, pack)

            tok[block, pl.ds(0, capacity), at] = share(block, at, capacity).astype(jnp.bfloat16)
            out_copy(block, index, way, False, True).start()

        @pl.when(jnp.logical_and(count > 0, index == 0))
        def _():
            rows_sent(block, 1 - way)

        @pl.when(count == 1)
        def _():
            @pl.when(index == 0)
            def _():
                picked[way, block] = packing(block, jnp.where(way == 0, exp - 1, exp + 1))

            out_copy(block, index, way, True, True).wait_recv()
            result = share(block, at) + unpacked(way, block, rx[block, pl.ds(0, capacity), at])
            tok[block, :, at] = result.astype(jnp.bfloat16)

        @pl.when(count > 1)
        def _():
            out_copy(block, index, way, True, False).wait_recv()
            result = share(block, at) + rx[block, :, at].astype(jnp.float32)
            tok[block, :, at] = result.astype(jnp.bfloat16)

        @pl.when(count > 0)
        def _():
            out_copy(block, index, way, False, False).start()

    def rows_sent(block, way):
        along = jnp.where(way == 0, up["expert"], dn["expert"])
        device = {"groups": grp, "expert": along}
        ref = tok.at[block]
        remote(ref, ref, tok_send.at[way, block], tok_recv.at[block, 0], device).wait_send()
        ref = gates.at[block]
        remote(ref, ref, gate_send.at[way, block], gate_recv.at[block], device).wait_send()

    def join(index, way, count):
        at = columns(index)
        slot = jnp.where(way == 0, exp, experts)

        @pl.when(count == 1)
        def _():
            @pl.when(index == 0)
            def _():
                picked[way, exp] = packing(exp, jnp.where(way == 0, exp - 1, exp + 1))

            out_copy(exp, index, way, True, True).wait_recv()
            acc[:, at] += unpacked(way, exp, rx[slot, pl.ds(0, capacity), at])

        @pl.when(count > 1)
        def _():
            out_copy(exp, index, way, True, False).wait_recv()
            acc[:, at] += rx[slot, :, at].astype(jnp.float32)

        out_ref[:, at] = acc[:, at].astype(jnp.bfloat16)

    period = out_pieces + SHIFT

    def after(far):
        return far // 2 * period + far % 2 * SHIFT + out_pieces

    defer = after(last - 1)

    def delay(count):
        return jnp.where(count == last, defer, LAG * count)

    near = LAG + after(last - 2) - NEAR_TICKS

    def until(count):
        end = delay(count) + after(jnp.where(count > 0, last - count, last - 1))
        return jnp.where(count == 1, near - (-out_pieces // NEAR), end)

    at_end = jnp.logical_or(exp == 0, exp == last)
    own_start = jnp.where(at_end, out_pieces, OWN_TICK - 1)

    def tick_job(tick):
        block, rest, due = exp, 1, tick == own_start
        for dist in (1, 2):
            first = (last - dist) // 2 * period + (last - dist) % 2 * SHIFT - 2
            away = jnp.where(exp == 0, dist, last - dist)
            begins = jnp.logical_and(at_end, tick == first)

            @pl.when(begins)
            def _():
                late_rows(away, dist)

            now = jnp.logical_and(at_end, jnp.logical_or(tick == first, tick == first + 1))
            block, rest = jnp.where(now, away, block), jnp.where(now, tick - first, rest)
            due = jnp.logical_or(due, now)

        def part(i):
            own = jnp.where(i == 0, mem, mem_c)
            hidden_part(block, jnp.where(rest == 0, own, (own + 2) % 4))

        @pl.when(due)
        def _():
            loop(2, part)

    def near_joins(tick):
        for way in range(2):
            for i in range(NEAR):
                index = (tick - near) * NEAR + i

                @pl.when(jnp.logical_and(behind[way] == 1, jnp.logical_and(index >= 0, index < out_pieces)))
                def _():
                    join(jnp.clip(index, 0, out_pieces - 1), way, behind[way])

    def role(tick, i):
        way = i % 2
        second = i // 2
        count = jnp.where(way == 0, exp, last - exp)
        ahead = last - count
        time = tick - delay(count)
        clock = jnp.maximum(time, 0)
        pair = clock // period
        index = clock % period - SHIFT * second
        far = 2 * pair + second
        dist = ahead - far
        block = jnp.clip(jnp.where(way == 0, exp + dist, exp - dist), 0, last)
        there = jnp.logical_and(time >= 0, jnp.logical_and(index >= 0, index < out_pieces))
        index = jnp.clip(index, 0, out_pieces - 1)

        @pl.when(jnp.logical_and(there, dist > 0))
        def _():
            send_result(block, index, way, count)

        @pl.when(jnp.logical_and(there, jnp.logical_and(dist == 0, count > 1)))
        def _():
            join(index, way, count)

    def second_tick(tick):
        @pl.when(tick < out_pieces)
        def _():
            down_there(jnp.minimum(tick, out_pieces - 1))

        loop(4, lambda i: role(tick, i))

        @pl.when(tick + AHEAD < out_pieces)
        def _():
            weight_tick(2, jnp.minimum(tick + AHEAD, out_pieces - 1))

        @pl.when(tick + LATE_DOWN < out_pieces)
        def _():
            weight_late(2, jnp.minimum(tick + LATE_DOWN, out_pieces - 1))

        tick_job(tick)
        turn = tick - own_start

        @pl.when(jnp.logical_and(turn >= 0, turn < out_pieces))
        def _():
            at = columns(jnp.clip(turn, 0, out_pieces - 1))
            acc[:, at] = res_ref[:, at].astype(jnp.float32) + share(exp, at)

        near_joins(tick)

    loop(jnp.maximum(until(behind[0]), until(behind[1])), second_tick)

    for way in range(2):

        @pl.when(onward[way])
        def _():
            rows_sent(exp, way)

    def results_sent(block):
        for way in range(2):
            passes = block > exp if way == 0 else block < exp
            for packed in (True, False):

                @pl.when(jnp.logical_and(passes, (behind[way] == 0) == packed))
                def _():
                    ref = tok.at[block, pl.ds(0, capacity if packed else rows)]
                    remote(ref, ref, ret_send.at[block], ret_recv.at[block, 0], (up, dn)[way]).wait_send()

    loop(experts, results_sent)
    for mat in range(3):
        c_copy(mat, False).wait_send()
        all_pieces(mat, y_send.at[mat], y_recv.at[mat], to_y).wait_send()
        all_pieces(mat, cy_send.at[mat], cy_recv.at[mat], to_c).wait_send()
        for i in range(groups - 1):
            device = {"groups": other(i), "expert": pos}
            all_pieces(mat, x_send.at[i, mat], x_recv.at[i, mat], device).wait_send()
            all_pieces(mat, cx_send.at[i, mat], cx_recv.at[i, mat], to_c).wait_send()


def shards(residual, norm_gain, router, w_gate, w_up, w_down, expert_ids):
    rows, width = residual.shape
    experts = router.shape[1]
    groups = lax.axis_size("groups")
    span = lax.axis_size("expert") // experts
    assert span == 4
    hid = w_gate.shape[1]
    capacity = 3 * rows * expert_ids.shape[1] // (2 * experts)
    capacity = min(rows, -(-capacity // 16) * 16)
    out_pieces = min(OUT_PIECES, width // (groups * LANES))
    w_pieces = W_PIECES
    while width // groups // w_pieces % 16:
        w_pieces //= 2
    vmem = pl.BlockSpec(memory_space=pltpu.VMEM)
    anywhere = pl.BlockSpec(memory_space=pl.ANY)
    dma = pltpu.SemaphoreType.DMA
    weight_copies = 2 * w_pieces + out_pieces
    return pl.pallas_call(
        functools.partial(kernel, groups, experts, span, capacity, out_pieces, w_pieces),
        out_shape=jax.ShapeDtypeStruct((rows, width), jnp.bfloat16),
        in_specs=[anywhere] * 7,
        out_specs=vmem,
        scratch_shapes=[
            pltpu.VMEM((rows, width), residual.dtype),
            pltpu.VMEM((1, width), norm_gain.dtype),
            pltpu.VMEM((experts, width), router.dtype),
            pltpu.VMEM(expert_ids.shape[::-1], expert_ids.dtype),
            pltpu.VMEM((experts, rows, width), jnp.bfloat16),
            pltpu.VMEM((experts, experts, rows), jnp.float32),
            pltpu.VMEM((span, experts, rows, hid), jnp.bfloat16),
            pltpu.VMEM((experts + 1, rows, width), jnp.bfloat16),
            pltpu.VMEM((rows, width), jnp.float32),
            pltpu.VMEM((2, experts, capacity, rows), jnp.bfloat16),
            pltpu.VMEM((span, width, hid), jnp.bfloat16),
            pltpu.VMEM((span, width, hid), jnp.bfloat16),
            pltpu.VMEM((span, hid, width), jnp.bfloat16),
            dma((4,)),
            dma((3,)),
            dma((experts, TOK_PIECES)),
            dma((2, experts)),
            dma((experts,)),
            dma((2, experts)),
            dma((experts,)),
            dma((experts + 1, out_pieces)),
            dma((3,)),
            dma((weight_copies,)),
            dma((groups - 1, 3)),
            dma((groups - 1, weight_copies)),
            dma((3,)),
            dma((3,)),
            dma((3,)),
            dma((2 + out_pieces,)),
            dma((groups - 1, 3)),
            dma((groups - 1, 2 + out_pieces)),
        ],
        compiler_params=pltpu.CompilerParams(
            collective_id=0, has_side_effects=True, vmem_limit_bytes=67043328
        ),
    )(residual, norm_gain[None], router.T, expert_ids.T, w_gate, w_up, w_down)


def solution(mesh):
    in_specs = (
        P(("groups", "expert"), None),
        P(),
        P(),
        P(None, "expert"),
        P(None, "expert"),
        P("expert", None),
        P(("groups", "expert"), None),
    )
    out_specs = P(("groups", "expert"), None)
    return jax.shard_map(shards, mesh=mesh, in_specs=in_specs, out_specs=out_specs, check_vma=False)
```

```python
import functools

import jax
import jax.numpy as jnp
from jax import lax
from jax.experimental import pallas as pl
from jax.experimental.pallas import tpu as pltpu
from jax.sharding import PartitionSpec as P

route_scale = 2.5
norm_eps = 1e-06
LANES = 128
MESH = pl.DeviceIdType.MESH

TOK_PIECES = 8
HEAD = 2
OUT_PIECES = 14
W_PIECES = 16
LAG = 2
SHIFT = 4
LATE = 2
AHEAD = 3
RELAYS = 3
JOINS = 3
JOIN_TICKS = 4
JOIN_LAG = 2
OWN_TICK = 5
OWN_START = 4


def kernel(
    groups,
    experts,
    span,
    capacity,
    out_pieces,
    w_pieces,
    res_in,
    gain_in,
    router_in,
    ids_in,
    wg_in,
    wu_in,
    wd_in,
    out_ref,
    res_ref,
    gain_ref,
    router_ref,
    ids_ref,
    tok,
    gates,
    act,
    rx,
    acc,
    picked,
    wg,
    wu,
    wd,
    in_sem,
    own_sem,
    land,
    tok_send,
    gate_recv,
    gate_send,
    ret_send,
    y_send,
    y_recv,
    x_send,
    x_recv,
    c_send,
    c_recv,
    cy_send,
    cy_recv,
    cx_send,
    cx_recv,
):
    rows, width = res_ref.shape
    grp = lax.axis_index("groups")
    pos = lax.axis_index("expert")
    exp = pos // span
    mem = pos % span
    last = experts - 1
    has_up = exp < last
    has_dn = exp > 0
    base = exp * span
    mem_y = (mem + 2) % 4
    mem_c = mem + 1 - 2 * (mem % 2)
    mem_yc = (mem_c + 2) % 4
    up = {"groups": grp, "expert": jnp.minimum(pos + span, experts * span - 1)}
    dn = {"groups": grp, "expert": jnp.maximum(pos - span, 0)}
    to_y = {"groups": grp, "expert": base + mem_y}
    to_c = {"groups": grp, "expert": base + mem_c}

    def other(i):
        return (grp + 1 + i) % groups

    barrier = pltpu.get_barrier_semaphore()

    def greet(device):
        pl.semaphore_signal(barrier, inc=1, device_id=device, device_id_type=MESH)

    greet(to_y)
    greet(to_c)
    for i in range(groups - 1):
        greet({"groups": other(i), "expert": pos})

    @pl.when(has_up)
    def _():
        greet(up)

    @pl.when(has_dn)
    def _():
        greet(dn)

    inputs = ((res_in, res_ref), (gain_in, gain_ref), (router_in, router_ref), (ids_in, ids_ref))
    loads = [pltpu.make_async_copy(*pair, in_sem.at[i]) for i, pair in enumerate(inputs)]
    for load in loads:
        load.start()

    mats = ((wg_in, wg), (wu_in, wu), (wd_in, wd))
    counts = (w_pieces, w_pieces, out_pieces)

    def piece(ref, mat, group, index):
        total = mats[mat][0].shape[mat // 2]
        size = total // groups // counts[mat]
        part = pl.ds(pl.multiple_of((index * groups + group) * size, size), size)
        return ref.at[:, part] if mat == 2 else ref.at[part]

    def number(mat, index):
        return sum(counts[:mat]) + index

    def remote(src, dst, send, recv, device):
        return pltpu.make_async_remote_copy(
            src_ref=src, dst_ref=dst, send_sem=send, recv_sem=recv, device_id=device, device_id_type=MESH
        )

    def y_copy(mat, index, landing):
        at = number(mat, index)
        ref = piece(mats[mat][1].at[mem_y if landing else mem], mat, grp, index)
        return remote(ref, ref, y_send.at[mat], y_recv.at[at], to_y)

    def x_copy(mat, index, i, landing):
        at = index if mat < 2 else w_pieces + index
        group = (grp + groups - 1 - i) % groups if landing else grp
        ref = piece(mats[mat][1].at[mem_y], mat, group, index)
        return remote(ref, ref, x_send.at[i, mat], x_recv.at[i, at], {"groups": other(i), "expert": pos})

    def landed(mat, index):
        return mat if mat < 2 else 2 + index

    def cy_copy(mat, index, landing):
        at = landed(mat, index)
        ref = piece(mats[mat][1].at[mem_yc if landing else mem_y], mat, grp, index)
        return remote(ref, ref, cy_send.at[mat], cy_recv.at[at], to_c)

    def cx_copy(mat, index, i, landing):
        at = landed(mat, index)
        group = (grp + groups - 1 - i) % groups
        ref = piece(mats[mat][1].at[mem_yc if landing else mem_y], mat, group, index)
        return remote(ref, ref, cx_send.at[i, mat], cx_recv.at[i, at], to_c)

    def all_pieces(mat, send, recv, device):
        ref = mats[mat][1].at[mem_y]
        part = pl.ds(0, mats[mat][0].shape[mat // 2] // groups)
        ref = ref.at[:, part] if mat == 2 else ref.at[part]
        return remote(ref, ref, send, recv, device)

    def c_copy(mat, landing):
        ref = mats[mat][1].at[mem_c if landing else mem]
        return remote(ref, ref, c_send.at[mat], c_recv.at[mat], to_c)

    def loop(count, body):
        def run(i, carry):
            body(i)
            return carry

        lax.fori_loop(0, count, run, 0)

    def start_pair(index):
        for mat in range(2):
            y_copy(mat, index, False).start()

    own_copies = [pltpu.make_async_copy(mats[i][0], mats[i][1].at[mem], own_sem.at[i]) for i in range(3)]
    for mat in range(3):
        own_copies[mat].start()

    step_rows = rows // TOK_PIECES
    tail = TOK_PIECES - HEAD
    ticks = (experts - 2) * TOK_PIECES
    behind = (exp, last - exp)
    onward = (has_up, has_dn)

    def tok_copy(block, index, way):
        ref = tok.at[block, pl.ds(pl.multiple_of(index * step_rows, step_rows), step_rows)]
        return remote(ref, ref, tok_send.at[way, block], land.at[block, index], (up, dn)[way])

    def gate_copy(block, way):
        ref = gates.at[block]
        return remote(ref, ref, gate_send.at[way, block], gate_recv.at[block], (up, dn)[way])

    def norm_rows(index):
        at = pl.ds(pl.multiple_of(index * step_rows, step_rows), step_rows)
        wide = res_ref[at, :].astype(jnp.float32)
        mean = jnp.mean(wide * wide, axis=1, keepdims=True)
        tok[exp, at, :] = (wide * lax.rsqrt(mean + norm_eps) * gain_ref[...].reshape(1, width)).astype(jnp.bfloat16)

    def first_rows(index):
        for way in range(2):
            early = jnp.logical_or(index < HEAD, behind[way] == 0)

            @pl.when(jnp.logical_and(onward[way], early))
            def _():
                tok_copy(exp, index, way).start()

    def gate_values():
        logits = lax.dot_general(
            router_ref[...], tok[exp], (((1,), (1,)), ((), ())), preferred_element_type=jnp.float32
        )
        affinity = jax.nn.sigmoid(logits)
        expert = lax.broadcasted_iota(jnp.int32, (experts, rows), 0)
        spread = jnp.zeros((experts, rows), jnp.float32)
        for k in range(ids_ref.shape[0]):
            spread = spread + jnp.where(expert == ids_ref[k : k + 1, :], affinity, 0.0)
        gates[exp] = route_scale * spread / jnp.sum(spread, axis=0, keepdims=True)

    peers = 1 + groups + has_up.astype(jnp.int32) + has_dn.astype(jnp.int32)
    pl.semaphore_wait(barrier, peers)
    for mat in range(2):
        own_copies[mat].wait()
    loop(w_pieces, start_pair)
    for load in loads:
        load.wait()

    def first_step(index):
        norm_rows(index)
        first_rows(index)

    loop(TOK_PIECES, first_step)
    own_copies[2].wait()
    loop(out_pieces, lambda index: y_copy(2, index, False).start())
    for mat in range(3):
        c_copy(mat, False).start()
    gate_values()
    for way in range(2):

        @pl.when(jnp.logical_and(onward[way], behind[way] == 0))
        def _():
            gate_copy(exp, way).start()

    def weight_tick(mat, index):
        y_copy(mat, index, True).wait_recv()
        for i in range(groups - 1):
            x_copy(mat, index, i, False).start()
        cy_copy(mat, index, False).start()

    def weight_late(index):
        for i in range(groups - 1):
            x_copy(2, index, i, True).wait_recv()
            cx_copy(2, index, i, False).start()

    def pair_late(index):
        both = wg.at[mem_y].at[pl.ds(0, 2 * (width // groups // w_pieces))]
        for i in range(groups - 1):
            device = {"groups": other(i), "expert": pos}
            remote(both, both, x_send.at[i, 0], x_recv.at[i, index], device).wait_recv()
            for mat in range(2):
                cx_copy(mat, index, i, False).start()

    def down_there(index):
        cy_copy(2, index, True).wait_recv()
        for i in range(groups - 1):
            cx_copy(2, index, i, True).wait_recv()

    def token_tick(step, way):
        tick = jnp.maximum(step, 0)
        count = behind[way]
        rest = jnp.maximum(tick - count * HEAD, 0)
        leading = tick < count * HEAD
        dist = jnp.where(leading, tick // HEAD + 1, count - rest // tail)
        dist = jnp.maximum(dist, 1)
        index = jnp.where(leading, tick % HEAD, HEAD + rest % tail)
        block = jnp.maximum(exp - dist, 0) if way == 0 else jnp.minimum(exp + dist, last)
        whole = index == TOK_PIECES - 1

        @pl.when(jnp.logical_and(step >= 0, tick < count * TOK_PIECES))
        def _():
            tok_copy(block, index, way).wait_recv()

            @pl.when(whole)
            def _():
                gate_copy(block, way).wait_recv()

            @pl.when(onward[way])
            def _():
                tok_copy(block, index, way).start()

                @pl.when(whole)
                def _():
                    gate_copy(block, way).start()

                @pl.when(tick == count * TOK_PIECES - 1)
                def _():
                    for own in range(HEAD, TOK_PIECES):
                        tok_copy(exp, own, way).start()
                    gate_copy(exp, way).start()

    def hidden_part(block, slot):
        rows_in = tok[block]
        gate_proj = jnp.dot(rows_in, wg[slot], preferred_element_type=jnp.float32)
        up_proj = jnp.dot(rows_in, wu[slot], preferred_element_type=jnp.float32)
        sublane = lax.broadcasted_iota(jnp.int32, (gates.shape[1], rows), 0)
        row = jnp.sum(jnp.where(sublane == exp, gates[block], 0.0), axis=0, keepdims=True)
        scale = jnp.broadcast_to(row, (LANES, rows)).T[:, :1]
        hidden = gate_proj / (1.0 + jnp.exp(-gate_proj)) * up_proj * scale
        act[slot, block] = hidden.astype(jnp.bfloat16)

    def whole_at(way, dist):
        count = behind[way]
        return count * HEAD + (count - dist + 1) * tail

    def found(tick, way):
        count = behind[way]
        over = tick + 1 - count * HEAD
        dist = count + 1 - over // tail
        there = jnp.logical_and(over > 0, over % tail == 0)
        return jnp.logical_and(there, jnp.logical_and(dist >= 1, dist <= count)), dist

    def first_tick(tick):
        @pl.when(tick < w_pieces)
        def _():
            weight_tick(0, tick)

        @pl.when(tick == w_pieces)
        def _():
            weight_tick(2, 0)

        token_tick(tick - 1, 0)
        token_tick(tick - 1, 1)

        @pl.when(tick < w_pieces)
        def _():
            weight_tick(1, tick)

        before = tick - LATE

        @pl.when(jnp.logical_and(before >= 0, before < w_pieces))
        def _():
            pair_late(jnp.maximum(before, 0))

        @pl.when(tick == OWN_TICK)
        def _():
            for mat in range(2):
                c_copy(mat, True).wait_recv()

        from_dn, dist_dn = found(tick - 1, 0)
        from_up, dist_up = found(tick - 1, 1)
        own = tick == OWN_TICK

        def job(i):
            side = i // 2
            slot = jnp.where(i % 2 == 0, mem, mem_c)
            block = jnp.where(side == 0, exp - dist_dn, jnp.where(side == 1, exp + dist_up, exp))
            valid = jnp.logical_or(
                jnp.logical_and(side == 0, from_dn),
                jnp.logical_or(jnp.logical_and(side == 1, from_up), jnp.logical_and(side == 2, own)),
            )

            @pl.when(valid)
            def _():
                hidden_part(jnp.clip(block, 0, last), slot)

        @pl.when(jnp.logical_or(own, jnp.logical_or(from_dn, from_up)))
        def _():
            loop(6, job)

    total = max(ticks, w_pieces) + 1
    loop(total, first_tick)
    rest = list(range(total - LATE, w_pieces))
    for index in range(max(len(rest), AHEAD - 1)):
        if index < len(rest):
            pair_late(rest[index])
        if 0 < index < AHEAD - 1:
            weight_tick(2, index)

    def far_job(first, i):
        dist = last - i // 2
        side = i % 2
        valid = False
        for way in range(2):
            full = jnp.logical_and(dist <= behind[way], whole_at(way, dist) <= ticks)
            valid = jnp.logical_or(valid, jnp.logical_and(side == way, full))
        block = jnp.where(side == 0, exp - dist, exp + dist)

        @pl.when(valid)
        def _():
            hidden_part(jnp.clip(block, 0, last), mem_y if first else mem_yc)

    def far_first(i):
        far_job(True, i)

        @pl.when(i == 1)
        def _():
            weight_late(0)

    def far_second(i):
        far_job(False, i)
        order = i // 2

        @pl.when(jnp.logical_and(i % 2 == 1, order < RELAYS))
        def _():
            weight_tick(2, AHEAD - 1 + jnp.minimum(order, RELAYS - 1))

    loop(2 * last, far_first)
    for mat in range(2):
        all_pieces(mat, cy_send.at[mat], cy_recv.at[mat], to_c).wait_recv()
        for i in range(groups - 1):
            all_pieces(mat, cx_send.at[i, mat], cx_recv.at[i, mat], to_c).wait_recv()
    loop(2 * last, far_second)
    weight_late(1)
    sent_on = AHEAD - 1 + RELAYS
    c_copy(2, True).wait_recv()

    cols = width // out_pieces

    def columns(index):
        return pl.ds(pl.multiple_of(index * cols, cols), cols)

    def out_copy(block, index, way, landing, packed):
        part = columns(index)
        height = pl.ds(0, capacity if packed else rows)
        target = exp if landing else exp - 1
        into = jnp.where(jnp.logical_and(way == 1, block == target), experts, block)
        along = jnp.where(way == 0, jnp.minimum(pos + span, experts * span - 1), jnp.maximum(pos - span, 0))
        return remote(
            tok.at[block, height, part],
            rx.at[into, height, part],
            ret_send.at[block],
            land.at[into, index],
            {"groups": grp, "expert": along},
        )

    def share(block, at, height=rows):
        part = pl.ds(0, height)
        result = jnp.dot(act[0, block, part], wd[0, :, at], preferred_element_type=jnp.float32)
        for slot in range(1, span):
            result = result + jnp.dot(act[slot, block, part], wd[slot, :, at], preferred_element_type=jnp.float32)
        return result

    def packing(block, expert):
        sublane = lax.broadcasted_iota(jnp.int32, (gates.shape[1], rows), 0)
        row = jnp.sum(jnp.where(sublane == expert, gates[block], 0.0), axis=0, keepdims=True)
        taken = jnp.broadcast_to(jnp.where(row != 0.0, 1.0, 0.0), (capacity, rows))
        source = lax.broadcasted_iota(jnp.int32, (rows, rows), 0)
        dest = lax.broadcasted_iota(jnp.int32, (rows, rows), 1)
        earlier = jnp.where(source < dest, 1.0, 0.0).astype(jnp.bfloat16)
        rank = jnp.dot(taken.astype(jnp.bfloat16), earlier, preferred_element_type=jnp.float32)
        slot = lax.broadcasted_iota(jnp.int32, (capacity, rows), 0).astype(jnp.float32)
        return jnp.where(rank == slot, taken, 0.0).astype(jnp.bfloat16)

    def unpacked(way, block, value):
        return lax.dot_general(
            picked[way, block], value, (((0,), (0,)), ((), ())), preferred_element_type=jnp.float32
        )

    def late_rows(block, dist):
        for index in range(HEAD, TOK_PIECES):

            @pl.when(jnp.logical_or(dist == 1, index >= TOK_PIECES - HEAD))
            def _():
                tok_copy(block, index, 0).wait_recv()

        gate_copy(block, 0).wait_recv()

    def send_result(block, index, way, count):
        at = columns(index)

        @pl.when(count == 0)
        def _():
            @pl.when(index == 0)
            def _():
                picks = packing(block, exp)

                def pack(slot):
                    act[slot, block, pl.ds(0, capacity)] = jnp.dot(
                        picks, act[slot, block], preferred_element_type=jnp.float32
                    ).astype(jnp.bfloat16)

                loop(span, pack)

            tok[block, pl.ds(0, capacity), at] = share(block, at, capacity).astype(jnp.bfloat16)
            out_copy(block, index, way, False, True).start()

        @pl.when(jnp.logical_and(count > 0, index == 0))
        def _():
            rows_sent(block, 1 - way)

        @pl.when(count == 1)
        def _():
            @pl.when(index == 0)
            def _():
                picked[way, block] = packing(block, jnp.where(way == 0, exp - 1, exp + 1))

            out_copy(block, index, way, True, True).wait_recv()
            result = share(block, at) + unpacked(way, block, rx[block, pl.ds(0, capacity), at])
            tok[block, :, at] = result.astype(jnp.bfloat16)

        @pl.when(count > 1)
        def _():
            out_copy(block, index, way, True, False).wait_recv()
            result = share(block, at) + rx[block, :, at].astype(jnp.float32)
            tok[block, :, at] = result.astype(jnp.bfloat16)

        @pl.when(count > 0)
        def _():
            out_copy(block, index, way, False, False).start()

    def rows_sent(block, way):
        along = jnp.where(way == 0, up["expert"], dn["expert"])
        device = {"groups": grp, "expert": along}
        ref = tok.at[block]
        remote(ref, ref, tok_send.at[way, block], land.at[block, 0], device).wait_send()
        ref = gates.at[block]
        remote(ref, ref, gate_send.at[way, block], gate_recv.at[block], device).wait_send()

    def join(index, way, count):
        at = columns(index)
        slot = jnp.where(way == 0, exp, experts)

        @pl.when(count == 1)
        def _():
            @pl.when(index == 0)
            def _():
                picked[way, exp] = packing(exp, jnp.where(way == 0, exp - 1, exp + 1))

            out_copy(exp, index, way, True, True).wait_recv()
            acc[:, at] += unpacked(way, exp, rx[slot, pl.ds(0, capacity), at])

        @pl.when(count > 1)
        def _():
            out_copy(exp, index, way, True, False).wait_recv()
            acc[:, at] += rx[slot, :, at].astype(jnp.float32)

        out_ref[:, at] = acc[:, at].astype(jnp.bfloat16)

    period = out_pieces + SHIFT

    def after(far):
        return far // 2 * period + far % 2 * SHIFT + out_pieces

    def joins(count):
        far = last - count
        start = LAG * count + far // 2 * period + far % 2 * SHIFT + JOIN_LAG
        start = jnp.where(count == last, after(last - 1), start)
        start = jnp.where(count == 1, LAG + after(last - 2) - JOIN_TICKS, start)
        rate = jnp.where(count == 1, JOINS, jnp.where(count == last, 2, 1))
        return start, rate

    def until(count):
        start, rate = joins(count)
        send_end = LAG * count + after(jnp.maximum(last - count - 1, 0))
        join_end = start + (out_pieces + rate - 1) // jnp.maximum(rate, 1)
        return jnp.maximum(jnp.where(count < last, send_end, 0), jnp.where(count > 0, join_end, 0))

    at_end = jnp.logical_or(exp == 0, exp == last)
    own_start = jnp.where(at_end, 2 * (period // 2 + 1), OWN_START)

    def tick_job(tick):
        block, slot, due = exp, jnp.where(tick == own_start, mem_y, mem_yc), tick // 2 == own_start // 2
        for dist in (1, 2):
            first = (last - dist) // 2 * period + (last - dist) % 2 * SHIFT - SHIFT
            away = jnp.where(exp == 0, dist, last - dist)
            begins = jnp.logical_and(at_end, tick == first)

            @pl.when(begins)
            def _():
                late_rows(away, dist)

            turn = tick - first
            now = jnp.logical_and(at_end, jnp.logical_and(turn >= 0, turn < span))
            block, slot = jnp.where(now, away, block), jnp.where(now, (mem + turn) % span, slot)
            due = jnp.logical_or(due, now)

        @pl.when(due)
        def _():
            hidden_part(block, slot)

    def join_tick(tick, way):
        count = behind[way]
        start, rate = joins(count)

        def one(i):
            index = (tick - start) * rate + i

            @pl.when(jnp.logical_and(index >= 0, index < out_pieces))
            def _():
                join(jnp.clip(index, 0, out_pieces - 1), way, count)

        @pl.when(jnp.logical_and(count > 0, tick >= start))
        def _():
            loop(rate, one)

    def role(tick, i):
        way = i % 2
        second = i // 2
        count = jnp.where(way == 0, exp, last - exp)
        ahead = last - count
        time = tick - LAG * count
        clock = jnp.maximum(time, 0)
        pair = clock // period
        index = clock % period - SHIFT * second
        far = 2 * pair + second
        dist = ahead - far
        block = jnp.clip(jnp.where(way == 0, exp + dist, exp - dist), 0, last)
        there = jnp.logical_and(time >= 0, jnp.logical_and(index >= 0, index < out_pieces))
        index = jnp.clip(index, 0, out_pieces - 1)

        @pl.when(jnp.logical_and(there, dist > 0))
        def _():
            send_result(block, index, way, count)

    def second_tick(tick):
        @pl.when(tick < out_pieces)
        def _():
            down_there(jnp.minimum(tick, out_pieces - 1))

        loop(4, lambda i: role(tick, i))

        @pl.when(tick + sent_on < out_pieces)
        def _():
            weight_tick(2, jnp.minimum(tick + sent_on, out_pieces - 1))

        @pl.when(tick + 2 < out_pieces)
        def _():
            weight_late(jnp.minimum(tick + 2, out_pieces - 1))

        tick_job(tick)
        turn = tick - own_start - 1

        @pl.when(jnp.logical_and(turn >= 0, turn < out_pieces))
        def _():
            at = columns(jnp.clip(turn, 0, out_pieces - 1))
            acc[:, at] = res_ref[:, at].astype(jnp.float32) + share(exp, at)

        join_tick(tick, 0)
        join_tick(tick, 1)

    loop(jnp.maximum(until(behind[0]), until(behind[1])), second_tick)

    for way in range(2):

        @pl.when(onward[way])
        def _():
            rows_sent(exp, way)

    def results_sent(block):
        for way in range(2):
            passes = block > exp if way == 0 else block < exp
            for packed in (True, False):

                @pl.when(jnp.logical_and(passes, (behind[way] == 0) == packed))
                def _():
                    ref = tok.at[block, pl.ds(0, capacity if packed else rows)]
                    remote(ref, ref, ret_send.at[block], land.at[block, 0], (up, dn)[way]).wait_send()

    loop(experts, results_sent)
    for mat in range(3):
        c_copy(mat, False).wait_send()
        all_pieces(mat, y_send.at[mat], y_recv.at[mat], to_y).wait_send()
        all_pieces(mat, cy_send.at[mat], cy_recv.at[mat], to_c).wait_send()
        for i in range(groups - 1):
            device = {"groups": other(i), "expert": pos}
            all_pieces(mat, x_send.at[i, mat], x_recv.at[i, mat], device).wait_send()
            all_pieces(mat, cx_send.at[i, mat], cx_recv.at[i, mat], to_c).wait_send()


def shards(residual, norm_gain, router, w_gate, w_up, w_down, expert_ids):
    rows, width = residual.shape
    experts = router.shape[1]
    groups = lax.axis_size("groups")
    span = lax.axis_size("expert") // experts
    assert span == 4
    hid = w_gate.shape[1]
    capacity = 3 * rows * expert_ids.shape[1] // (2 * experts)
    capacity = min(rows, -(-capacity // 16) * 16)
    out_pieces = min(OUT_PIECES, width // (groups * LANES))
    w_pieces = W_PIECES
    while width // groups // w_pieces % 16:
        w_pieces //= 2
    vmem = pl.BlockSpec(memory_space=pltpu.VMEM)
    anywhere = pl.BlockSpec(memory_space=pl.ANY)
    dma = pltpu.SemaphoreType.DMA
    weight_copies = 2 * w_pieces + out_pieces
    return pl.pallas_call(
        functools.partial(kernel, groups, experts, span, capacity, out_pieces, w_pieces),
        out_shape=pltpu.VMEM((rows, width), jnp.bfloat16),
        in_specs=[anywhere] * 7,
        out_specs=vmem,
        scratch_shapes=[
            pltpu.VMEM((rows, width), residual.dtype),
            pltpu.VMEM((width,), norm_gain.dtype),
            pltpu.VMEM((experts, width), router.dtype),
            pltpu.VMEM(expert_ids.shape[::-1], expert_ids.dtype),
            pltpu.VMEM((experts, rows, width), jnp.bfloat16),
            pltpu.VMEM((experts, experts, rows), jnp.float32),
            pltpu.VMEM((span, experts, rows, hid), jnp.bfloat16),
            pltpu.VMEM((experts + 1, rows, width), jnp.bfloat16),
            pltpu.VMEM((rows, width), jnp.float32),
            pltpu.VMEM((2, experts, capacity, rows), jnp.bfloat16),
            pltpu.VMEM((span, width, hid), jnp.bfloat16),
            pltpu.VMEM((span, width, hid), jnp.bfloat16),
            pltpu.VMEM((span, hid, width), jnp.bfloat16),
            dma((4,)),
            dma((3,)),
            dma((experts + 1, max(TOK_PIECES, out_pieces))),
            dma((2, experts)),
            dma((experts,)),
            dma((2, experts)),
            dma((experts,)),
            dma((3,)),
            dma((weight_copies,)),
            dma((groups - 1, 3)),
            dma((groups - 1, w_pieces + out_pieces)),
            dma((3,)),
            dma((3,)),
            dma((3,)),
            dma((2 + out_pieces,)),
            dma((groups - 1, 3)),
            dma((groups - 1, 2 + out_pieces)),
        ],
        compiler_params=pltpu.CompilerParams(
            collective_id=0, has_side_effects=True, vmem_limit_bytes=67043328 - 2 * rows * width
        ),
    )(residual, norm_gain, router.T, expert_ids.T, w_gate, w_up, w_down)


def solution(mesh):
    in_specs = (
        P(("groups", "expert"), None),
        P(),
        P(),
        P(None, "expert"),
        P(None, "expert"),
        P("expert", None),
        P(("groups", "expert"), None),
    )
    out_specs = P(("groups", "expert"), None)
    return jax.shard_map(shards, mesh=mesh, in_specs=in_specs, out_specs=out_specs, check_vma=False)
```

```python
import functools

import jax
import jax.numpy as jnp
from jax import lax
from jax.experimental import pallas as pl
from jax.experimental.pallas import tpu as pltpu
from jax.sharding import PartitionSpec as P

route_scale = 2.5
norm_eps = 1e-06
LANES = 128
MESH = pl.DeviceIdType.MESH

TOK_PIECES = 8
HEAD = 2
OUT_PIECES = 14
W_PIECES = 16
LAG = 2
SHIFT = 4
LATE = 2
AHEAD = 3
RELAYS = 1
JOINS = 3
JOIN_TICKS = 4
JOIN_LAG = 2
OWN_TICK = 5
OWN_START = 4


def kernel(
    groups,
    experts,
    span,
    capacity,
    out_pieces,
    w_pieces,
    res_in,
    gain_in,
    router_in,
    ids_in,
    wg_in,
    wu_in,
    wd_in,
    out_ref,
    res_ref,
    gain_ref,
    router_ref,
    ids_ref,
    tok,
    gates,
    act,
    rx,
    acc,
    picked,
    wg,
    wu,
    wd,
    in_sem,
    own_sem,
    land,
    tok_send,
    gate_recv,
    gate_send,
    ret_send,
    y_send,
    y_recv,
    x_send,
    x_recv,
    c_send,
    c_recv,
    cy_send,
    cy_recv,
    cx_send,
    cx_recv,
):
    rows, width = res_ref.shape
    grp = lax.axis_index("groups")
    pos = lax.axis_index("expert")
    exp = pos // span
    mem = pos % span
    last = experts - 1
    has_up = exp < last
    has_dn = exp > 0
    base = exp * span
    mem_y = (mem + 2) % 4
    mem_c = mem + 1 - 2 * (mem % 2)
    mem_yc = (mem_c + 2) % 4
    up = {"groups": grp, "expert": jnp.minimum(pos + span, experts * span - 1)}
    dn = {"groups": grp, "expert": jnp.maximum(pos - span, 0)}
    to_y = {"groups": grp, "expert": base + mem_y}
    to_c = {"groups": grp, "expert": base + mem_c}

    def other(i):
        return (grp + 1 + i) % groups

    barrier = pltpu.get_barrier_semaphore()

    def greet(device):
        pl.semaphore_signal(barrier, inc=1, device_id=device, device_id_type=MESH)

    greet(to_y)
    greet(to_c)
    for i in range(groups - 1):
        greet({"groups": other(i), "expert": pos})

    @pl.when(has_up)
    def _():
        greet(up)

    @pl.when(has_dn)
    def _():
        greet(dn)

    inputs = ((res_in, res_ref), (gain_in, gain_ref), (router_in, router_ref), (ids_in, ids_ref))
    loads = [pltpu.make_async_copy(*pair, in_sem.at[i]) for i, pair in enumerate(inputs)]
    for load in loads:
        load.start()

    mats = ((wg_in, wg), (wu_in, wu), (wd_in, wd))
    counts = (w_pieces, w_pieces, out_pieces)

    def piece(ref, mat, group, index):
        total = mats[mat][0].shape[mat // 2]
        size = total // groups // counts[mat]
        part = pl.ds(pl.multiple_of((index * groups + group) * size, size), size)
        return ref.at[:, part] if mat == 2 else ref.at[part]

    def number(mat, index):
        return sum(counts[:mat]) + index

    def remote(src, dst, send, recv, device):
        return pltpu.make_async_remote_copy(
            src_ref=src, dst_ref=dst, send_sem=send, recv_sem=recv, device_id=device, device_id_type=MESH
        )

    def y_copy(mat, index, landing):
        at = number(mat, index)
        ref = piece(mats[mat][1].at[mem_y if landing else mem], mat, grp, index)
        return remote(ref, ref, y_send.at[mat], y_recv.at[at], to_y)

    def x_copy(mat, index, i, landing):
        at = index if mat < 2 else w_pieces + index
        group = (grp + groups - 1 - i) % groups if landing else grp
        ref = piece(mats[mat][1].at[mem_y], mat, group, index)
        return remote(ref, ref, x_send.at[i, mat], x_recv.at[i, at], {"groups": other(i), "expert": pos})

    def landed(mat, index):
        return mat if mat < 2 else 2 + index

    def cy_copy(mat, index, landing):
        at = landed(mat, index)
        ref = piece(mats[mat][1].at[mem_yc if landing else mem_y], mat, grp, index)
        return remote(ref, ref, cy_send.at[mat], cy_recv.at[at], to_c)

    def cx_copy(mat, index, i, landing):
        at = landed(mat, index)
        group = (grp + groups - 1 - i) % groups
        ref = piece(mats[mat][1].at[mem_yc if landing else mem_y], mat, group, index)
        return remote(ref, ref, cx_send.at[i, mat], cx_recv.at[i, at], to_c)

    def all_pieces(mat, send, recv, device):
        ref = mats[mat][1].at[mem_y]
        part = pl.ds(0, mats[mat][0].shape[mat // 2] // groups)
        ref = ref.at[:, part] if mat == 2 else ref.at[part]
        return remote(ref, ref, send, recv, device)

    def c_copy(mat, landing):
        ref = mats[mat][1].at[mem_c if landing else mem]
        return remote(ref, ref, c_send.at[mat], c_recv.at[mat], to_c)

    def loop(count, body):
        def run(i, carry):
            body(i)
            return carry

        lax.fori_loop(0, count, run, 0)

    def start_pair(index):
        for mat in range(2):
            y_copy(mat, index, False).start()

    own_copies = [pltpu.make_async_copy(mats[i][0], mats[i][1].at[mem], own_sem.at[i]) for i in range(3)]
    for mat in range(3):
        own_copies[mat].start()

    step_rows = rows // TOK_PIECES
    tail = TOK_PIECES - HEAD
    ticks = (experts - 2) * TOK_PIECES
    behind = (exp, last - exp)
    onward = (has_up, has_dn)

    def tok_copy(block, index, way):
        ref = tok.at[block, pl.ds(pl.multiple_of(index * step_rows, step_rows), step_rows)]
        return remote(ref, ref, tok_send.at[way, block], land.at[block, index], (up, dn)[way])

    def gate_copy(block, way):
        ref = gates.at[block]
        return remote(ref, ref, gate_send.at[way, block], gate_recv.at[block], (up, dn)[way])

    def norm_rows(index):
        at = pl.ds(pl.multiple_of(index * step_rows, step_rows), step_rows)
        wide = res_ref[at, :].astype(jnp.float32)
        mean = jnp.mean(wide * wide, axis=1, keepdims=True)
        tok[exp, at, :] = (wide * lax.rsqrt(mean + norm_eps) * gain_ref[...].reshape(1, width)).astype(jnp.bfloat16)

    def first_rows(index):
        for way in range(2):
            early = jnp.logical_or(index < HEAD, behind[way] == 0)

            @pl.when(jnp.logical_and(onward[way], early))
            def _():
                tok_copy(exp, index, way).start()

    def gate_values():
        logits = lax.dot_general(
            router_ref[...], tok[exp], (((1,), (1,)), ((), ())), preferred_element_type=jnp.float32
        )
        affinity = jax.nn.sigmoid(logits)
        expert = lax.broadcasted_iota(jnp.int32, (experts, rows), 0)
        spread = jnp.zeros((experts, rows), jnp.float32)
        for k in range(ids_ref.shape[0]):
            spread = spread + jnp.where(expert == ids_ref[k : k + 1, :], affinity, 0.0)
        gates[exp] = route_scale * spread / jnp.sum(spread, axis=0, keepdims=True)

    peers = 1 + groups + has_up.astype(jnp.int32) + has_dn.astype(jnp.int32)
    pl.semaphore_wait(barrier, peers)
    for mat in range(2):
        own_copies[mat].wait()
    loop(w_pieces, start_pair)
    for load in loads:
        load.wait()

    def first_step(index):
        norm_rows(index)
        first_rows(index)

    loop(TOK_PIECES, first_step)
    own_copies[2].wait()
    loop(out_pieces, lambda index: y_copy(2, index, False).start())
    for mat in range(3):
        c_copy(mat, False).start()
    gate_values()
    for way in range(2):

        @pl.when(jnp.logical_and(onward[way], behind[way] == 0))
        def _():
            gate_copy(exp, way).start()

    def weight_tick(mat, index):
        y_copy(mat, index, True).wait_recv()
        for i in range(groups - 1):
            x_copy(mat, index, i, False).start()
        cy_copy(mat, index, False).start()

    def weight_late(index):
        for i in range(groups - 1):
            x_copy(2, index, i, True).wait_recv()
            cx_copy(2, index, i, False).start()

    def pair_late(index):
        both = wg.at[mem_y].at[pl.ds(0, 2 * (width // groups // w_pieces))]
        for i in range(groups - 1):
            device = {"groups": other(i), "expert": pos}
            remote(both, both, x_send.at[i, 0], x_recv.at[i, index], device).wait_recv()
            for mat in range(2):
                cx_copy(mat, index, i, False).start()

    def down_there(index):
        cy_copy(2, index, True).wait_recv()
        for i in range(groups - 1):
            cx_copy(2, index, i, True).wait_recv()

    def token_tick(step, way):
        tick = jnp.maximum(step, 0)
        count = behind[way]
        rest = jnp.maximum(tick - count * HEAD, 0)
        leading = tick < count * HEAD
        dist = jnp.where(leading, tick // HEAD + 1, count - rest // tail)
        dist = jnp.maximum(dist, 1)
        index = jnp.where(leading, tick % HEAD, HEAD + rest % tail)
        block = jnp.maximum(exp - dist, 0) if way == 0 else jnp.minimum(exp + dist, last)
        whole = index == TOK_PIECES - 1

        @pl.when(jnp.logical_and(step >= 0, tick < count * TOK_PIECES))
        def _():
            tok_copy(block, index, way).wait_recv()

            @pl.when(whole)
            def _():
                gate_copy(block, way).wait_recv()

            @pl.when(onward[way])
            def _():
                tok_copy(block, index, way).start()

                @pl.when(whole)
                def _():
                    gate_copy(block, way).start()

                @pl.when(tick == count * TOK_PIECES - 1)
                def _():
                    for own in range(HEAD, TOK_PIECES):
                        tok_copy(exp, own, way).start()
                    gate_copy(exp, way).start()

    def hidden_part(block, slot):
        rows_in = tok[block]
        gate_proj = jnp.dot(rows_in, wg[slot], preferred_element_type=jnp.float32)
        up_proj = jnp.dot(rows_in, wu[slot], preferred_element_type=jnp.float32)
        sublane = lax.broadcasted_iota(jnp.int32, (gates.shape[1], rows), 0)
        row = jnp.sum(jnp.where(sublane == exp, gates[block], 0.0), axis=0, keepdims=True)
        scale = jnp.broadcast_to(row, (LANES, rows)).T[:, :1]
        hidden = gate_proj / (1.0 + jnp.exp(-gate_proj)) * up_proj * scale
        act[slot, block] = hidden.astype(jnp.bfloat16)

    def whole_at(way, dist):
        count = behind[way]
        return count * HEAD + (count - dist + 1) * tail

    def found(tick, way):
        count = behind[way]
        over = tick + 1 - count * HEAD
        dist = count + 1 - over // tail
        there = jnp.logical_and(over > 0, over % tail == 0)
        return jnp.logical_and(there, jnp.logical_and(dist >= 1, dist <= count)), dist

    def first_tick(tick):
        @pl.when(tick < w_pieces)
        def _():
            weight_tick(0, tick)

        @pl.when(tick == w_pieces)
        def _():
            weight_tick(2, 0)

        token_tick(tick - 1, 0)
        token_tick(tick - 1, 1)

        @pl.when(tick < w_pieces)
        def _():
            weight_tick(1, tick)

        before = tick - LATE

        @pl.when(jnp.logical_and(before >= 0, before < w_pieces))
        def _():
            pair_late(jnp.maximum(before, 0))

        @pl.when(tick == OWN_TICK)
        def _():
            for mat in range(2):
                c_copy(mat, True).wait_recv()

        from_dn, dist_dn = found(tick - 1, 0)
        from_up, dist_up = found(tick - 1, 1)
        own = tick == OWN_TICK

        def job(i):
            side = i // 2
            slot = jnp.where(i % 2 == 0, mem, mem_c)
            block = jnp.where(side == 0, exp - dist_dn, jnp.where(side == 1, exp + dist_up, exp))
            valid = jnp.logical_or(
                jnp.logical_and(side == 0, from_dn),
                jnp.logical_or(jnp.logical_and(side == 1, from_up), jnp.logical_and(side == 2, own)),
            )

            @pl.when(valid)
            def _():
                hidden_part(jnp.clip(block, 0, last), slot)

        @pl.when(jnp.logical_or(own, jnp.logical_or(from_dn, from_up)))
        def _():
            loop(6, job)

    def packing(block, expert):
        sublane = lax.broadcasted_iota(jnp.int32, (gates.shape[1], rows), 0)
        row = jnp.sum(jnp.where(sublane == expert, gates[block], 0.0), axis=0, keepdims=True)
        taken = jnp.broadcast_to(jnp.where(row != 0.0, 1.0, 0.0), (capacity, rows))
        source = lax.broadcasted_iota(jnp.int32, (rows, rows), 0)
        dest = lax.broadcasted_iota(jnp.int32, (rows, rows), 1)
        earlier = jnp.where(source < dest, 1.0, 0.0).astype(jnp.bfloat16)
        rank = jnp.dot(taken.astype(jnp.bfloat16), earlier, preferred_element_type=jnp.float32)
        slot = lax.broadcasted_iota(jnp.int32, (capacity, rows), 0).astype(jnp.float32)
        return jnp.where(rank == slot, taken, 0.0).astype(jnp.bfloat16)

    at_end = jnp.logical_or(exp == 0, exp == last)

    end_way = jnp.where(exp == 0, 0, 1)

    def pick(block):
        picked[end_way, block] = packing(block, exp)

    def pack(block, slot):
        act[slot, block, pl.ds(0, capacity)] = jnp.dot(
            picked[end_way, block], act[slot, block], preferred_element_type=jnp.float32
        ).astype(jnp.bfloat16)

    def pick_far(i):
        block = jnp.where(exp == 0, last - i, i)
        pick(block)
        pack(block, mem)
        pack(block, mem_c)

    total = max(ticks, w_pieces) + 1
    loop(total, first_tick)
    rest = list(range(total - LATE, w_pieces))
    weight_tick(2, 1)

    @pl.when(at_end)
    def _():
        loop(last - 2, pick_far)

    for index in rest:
        pair_late(index)
    weight_tick(2, 2)

    def far_job(first, i):
        dist = last - i // 2
        side = i % 2
        valid = False
        for way in range(2):
            full = jnp.logical_and(dist <= behind[way], whole_at(way, dist) <= ticks)
            valid = jnp.logical_or(valid, jnp.logical_and(side == way, full))
        block = jnp.where(side == 0, exp - dist, exp + dist)

        @pl.when(valid)
        def _():
            slot = mem_y if first else mem_yc
            hidden_part(jnp.clip(block, 0, last), slot)

            @pl.when(at_end)
            def _():
                pack(jnp.clip(block, 0, last), slot)

    def far_first(i):
        far_job(True, i)

        @pl.when(i == 1)
        def _():
            weight_late(0)

    def far_second(i):
        far_job(False, i)
        order = i // 2

        @pl.when(jnp.logical_and(i % 2 == 1, order < RELAYS))
        def _():
            weight_tick(2, AHEAD + jnp.minimum(order, RELAYS - 1))

    loop(2 * last, far_first)
    for mat in range(2):
        all_pieces(mat, cy_send.at[mat], cy_recv.at[mat], to_c).wait_recv()
        for i in range(groups - 1):
            all_pieces(mat, cx_send.at[i, mat], cx_recv.at[i, mat], to_c).wait_recv()
    loop(2 * last, far_second)
    weight_late(1)
    sent_on = AHEAD + RELAYS
    c_copy(2, True).wait_recv()

    cols = width // out_pieces

    def columns(index):
        return pl.ds(pl.multiple_of(index * cols, cols), cols)

    def out_copy(block, index, way, landing, packed):
        part = columns(index)
        height = pl.ds(0, capacity if packed else rows)
        target = exp if landing else exp - 1
        into = jnp.where(jnp.logical_and(way == 1, block == target), experts, block)
        along = jnp.where(way == 0, jnp.minimum(pos + span, experts * span - 1), jnp.maximum(pos - span, 0))
        return remote(
            tok.at[block, height, part],
            rx.at[into, height, part],
            ret_send.at[block],
            land.at[into, index],
            {"groups": grp, "expert": along},
        )

    def share(block, at, height=rows):
        part = pl.ds(0, height)
        result = jnp.dot(act[0, block, part], wd[0, :, at], preferred_element_type=jnp.float32)
        for slot in range(1, span):
            result = result + jnp.dot(act[slot, block, part], wd[slot, :, at], preferred_element_type=jnp.float32)
        return result

    def unpacked(way, block, value):
        return lax.dot_general(
            picked[way, block], value, (((0,), (0,)), ((), ())), preferred_element_type=jnp.float32
        )

    def late_rows(block, dist):
        for index in range(HEAD, TOK_PIECES):

            @pl.when(jnp.logical_or(dist == 1, index >= TOK_PIECES - HEAD))
            def _():
                tok_copy(block, index, 0).wait_recv()

        gate_copy(block, 0).wait_recv()
        pick(block)

    def send_result(block, index, way, count):
        at = columns(index)

        @pl.when(count == 0)
        def _():
            tok[block, pl.ds(0, capacity), at] = share(block, at, capacity).astype(jnp.bfloat16)
            out_copy(block, index, way, False, True).start()

        @pl.when(jnp.logical_and(count > 0, index == 0))
        def _():
            rows_sent(block, 1 - way)

        @pl.when(count == 1)
        def _():
            @pl.when(index == 0)
            def _():
                picked[way, block] = packing(block, jnp.where(way == 0, exp - 1, exp + 1))

            out_copy(block, index, way, True, True).wait_recv()
            result = share(block, at) + unpacked(way, block, rx[block, pl.ds(0, capacity), at])
            tok[block, :, at] = result.astype(jnp.bfloat16)

        @pl.when(count > 1)
        def _():
            out_copy(block, index, way, True, False).wait_recv()
            result = share(block, at) + rx[block, :, at].astype(jnp.float32)
            tok[block, :, at] = result.astype(jnp.bfloat16)

        @pl.when(count > 0)
        def _():
            out_copy(block, index, way, False, False).start()

    def rows_sent(block, way):
        along = jnp.where(way == 0, up["expert"], dn["expert"])
        device = {"groups": grp, "expert": along}
        ref = tok.at[block]
        remote(ref, ref, tok_send.at[way, block], land.at[block, 0], device).wait_send()
        ref = gates.at[block]
        remote(ref, ref, gate_send.at[way, block], gate_recv.at[block], device).wait_send()

    def join(index, way, count):
        at = columns(index)
        slot = jnp.where(way == 0, exp, experts)

        @pl.when(count == 1)
        def _():
            @pl.when(index == 0)
            def _():
                picked[way, exp] = packing(exp, jnp.where(way == 0, exp - 1, exp + 1))

            out_copy(exp, index, way, True, True).wait_recv()
            acc[:, at] += unpacked(way, exp, rx[slot, pl.ds(0, capacity), at])

        @pl.when(count > 1)
        def _():
            out_copy(exp, index, way, True, False).wait_recv()
            acc[:, at] += rx[slot, :, at].astype(jnp.float32)

        out_ref[:, at] = acc[:, at].astype(jnp.bfloat16)

    period = out_pieces + SHIFT

    def after(far):
        return far // 2 * period + far % 2 * SHIFT + out_pieces

    def joins(count):
        far = last - count
        start = LAG * count + far // 2 * period + far % 2 * SHIFT + JOIN_LAG
        start = jnp.where(count == last, after(last - 1), start)
        start = jnp.where(count == 1, LAG + after(last - 2) - JOIN_TICKS, start)
        rate = jnp.where(count == 1, JOINS, jnp.where(count == last, 2, 1))
        return start, rate

    def until(count):
        start, rate = joins(count)
        send_end = LAG * count + after(jnp.maximum(last - count - 1, 0))
        join_end = start + (out_pieces + rate - 1) // jnp.maximum(rate, 1)
        return jnp.maximum(jnp.where(count < last, send_end, 0), jnp.where(count > 0, join_end, 0))

    own_start = jnp.where(at_end, 2 * (period // 2 + 1), OWN_START)

    def tick_job(tick):
        block, slot, due = exp, jnp.where(tick == own_start, mem_y, mem_yc), tick // 2 == own_start // 2
        for dist in (1, 2):
            first = (last - dist) // 2 * period + (last - dist) % 2 * SHIFT - SHIFT
            away = jnp.where(exp == 0, dist, last - dist)
            begins = jnp.logical_and(at_end, tick == first)

            @pl.when(begins)
            def _():
                late_rows(away, dist)

            turn = tick - first
            now = jnp.logical_and(at_end, jnp.logical_and(turn >= 0, turn < span))
            block, slot = jnp.where(now, away, block), jnp.where(now, (mem + turn) % span, slot)
            due = jnp.logical_or(due, now)

        @pl.when(due)
        def _():
            hidden_part(block, slot)

            @pl.when(block != exp)
            def _():
                pack(block, slot)

    def join_tick(tick, way):
        count = behind[way]
        start, rate = joins(count)

        def one(i):
            index = (tick - start) * rate + i

            @pl.when(jnp.logical_and(index >= 0, index < out_pieces))
            def _():
                join(jnp.clip(index, 0, out_pieces - 1), way, count)

        @pl.when(jnp.logical_and(count > 0, tick >= start))
        def _():
            loop(rate, one)

    def role(tick, i):
        way = i % 2
        second = i // 2
        count = jnp.where(way == 0, exp, last - exp)
        ahead = last - count
        time = tick - LAG * count
        clock = jnp.maximum(time, 0)
        pair = clock // period
        index = clock % period - SHIFT * second
        far = 2 * pair + second
        dist = ahead - far
        block = jnp.clip(jnp.where(way == 0, exp + dist, exp - dist), 0, last)
        there = jnp.logical_and(time >= 0, jnp.logical_and(index >= 0, index < out_pieces))
        index = jnp.clip(index, 0, out_pieces - 1)

        @pl.when(jnp.logical_and(there, dist > 0))
        def _():
            send_result(block, index, way, count)

    def second_tick(tick):
        @pl.when(tick < out_pieces)
        def _():
            down_there(jnp.minimum(tick, out_pieces - 1))

        loop(4, lambda i: role(tick, i))
        tick_job(tick)

        @pl.when(tick + sent_on < out_pieces)
        def _():
            weight_tick(2, jnp.minimum(tick + sent_on, out_pieces - 1))

        @pl.when(tick + 2 < out_pieces)
        def _():
            weight_late(jnp.minimum(tick + 2, out_pieces - 1))

        turn = tick - own_start - 1

        @pl.when(jnp.logical_and(turn >= 0, turn < out_pieces))
        def _():
            at = columns(jnp.clip(turn, 0, out_pieces - 1))
            acc[:, at] = res_ref[:, at].astype(jnp.float32) + share(exp, at)

        join_tick(tick, 0)
        join_tick(tick, 1)

    loop(jnp.maximum(until(behind[0]), until(behind[1])), second_tick)

    for way in range(2):

        @pl.when(onward[way])
        def _():
            rows_sent(exp, way)

    def results_sent(block):
        for way in range(2):
            passes = block > exp if way == 0 else block < exp
            for packed in (True, False):

                @pl.when(jnp.logical_and(passes, (behind[way] == 0) == packed))
                def _():
                    ref = tok.at[block, pl.ds(0, capacity if packed else rows)]
                    remote(ref, ref, ret_send.at[block], land.at[block, 0], (up, dn)[way]).wait_send()

    loop(experts, results_sent)
    for mat in range(3):
        c_copy(mat, False).wait_send()
        all_pieces(mat, y_send.at[mat], y_recv.at[mat], to_y).wait_send()
        all_pieces(mat, cy_send.at[mat], cy_recv.at[mat], to_c).wait_send()
        for i in range(groups - 1):
            device = {"groups": other(i), "expert": pos}
            all_pieces(mat, x_send.at[i, mat], x_recv.at[i, mat], device).wait_send()
            all_pieces(mat, cx_send.at[i, mat], cx_recv.at[i, mat], to_c).wait_send()


def shards(residual, norm_gain, router, w_gate, w_up, w_down, expert_ids):
    rows, width = residual.shape
    experts = router.shape[1]
    groups = lax.axis_size("groups")
    span = lax.axis_size("expert") // experts
    assert span == 4
    hid = w_gate.shape[1]
    capacity = 3 * rows * expert_ids.shape[1] // (2 * experts)
    capacity = min(rows, -(-capacity // 16) * 16)
    out_pieces = min(OUT_PIECES, width // (groups * LANES))
    w_pieces = W_PIECES
    while width // groups // w_pieces % 16:
        w_pieces //= 2
    vmem = pl.BlockSpec(memory_space=pltpu.VMEM)
    anywhere = pl.BlockSpec(memory_space=pl.ANY)
    dma = pltpu.SemaphoreType.DMA
    weight_copies = 2 * w_pieces + out_pieces
    return pl.pallas_call(
        functools.partial(kernel, groups, experts, span, capacity, out_pieces, w_pieces),
        out_shape=pltpu.VMEM((rows, width), jnp.bfloat16),
        in_specs=[anywhere] * 7,
        out_specs=vmem,
        scratch_shapes=[
            pltpu.VMEM((rows, width), residual.dtype),
            pltpu.VMEM((width,), norm_gain.dtype),
            pltpu.VMEM((experts, width), router.dtype),
            pltpu.VMEM(expert_ids.shape[::-1], expert_ids.dtype),
            pltpu.VMEM((experts, rows, width), jnp.bfloat16),
            pltpu.VMEM((experts, experts, rows), jnp.float32),
            pltpu.VMEM((span, experts, rows, hid), jnp.bfloat16),
            pltpu.VMEM((experts + 1, rows, width), jnp.bfloat16),
            pltpu.VMEM((rows, width), jnp.float32),
            pltpu.VMEM((2, experts, capacity, rows), jnp.bfloat16),
            pltpu.VMEM((span, width, hid), jnp.bfloat16),
            pltpu.VMEM((span, width, hid), jnp.bfloat16),
            pltpu.VMEM((span, hid, width), jnp.bfloat16),
            dma((4,)),
            dma((3,)),
            dma((experts + 1, max(TOK_PIECES, out_pieces))),
            dma((2, experts)),
            dma((experts,)),
            dma((2, experts)),
            dma((experts,)),
            dma((3,)),
            dma((weight_copies,)),
            dma((groups - 1, 3)),
            dma((groups - 1, w_pieces + out_pieces)),
            dma((3,)),
            dma((3,)),
            dma((3,)),
            dma((2 + out_pieces,)),
            dma((groups - 1, 3)),
            dma((groups - 1, 2 + out_pieces)),
        ],
        compiler_params=pltpu.CompilerParams(
            collective_id=0, has_side_effects=True, vmem_limit_bytes=67043328 - 2 * rows * width
        ),
    )(residual, norm_gain, router.T, expert_ids.T, w_gate, w_up, w_down)


def solution(mesh):
    in_specs = (
        P(("groups", "expert"), None),
        P(),
        P(),
        P(None, "expert"),
        P(None, "expert"),
        P("expert", None),
        P(("groups", "expert"), None),
    )
    out_specs = P(("groups", "expert"), None)
    return jax.shard_map(shards, mesh=mesh, in_specs=in_specs, out_specs=out_specs, check_vma=False)
```

```python
import functools

import jax
import jax.numpy as jnp
from jax import lax
from jax.experimental import pallas as pl
from jax.experimental.pallas import tpu as pltpu
from jax.sharding import PartitionSpec as P

route_scale = 2.5
norm_eps = 1e-06
LANES = 128
MESH = pl.DeviceIdType.MESH

TOK_PIECES = 8
HEAD = 2
OUT_PIECES = 14
W_PIECES = 16
LAG = 2
SHIFT = 4
LATE = 2
AHEAD = 3
RELAYS = 1
JOINS = 3
JOIN_TICKS = 3
JOIN_LAG = 2
OWN_TICK = 5
OWN_START = 4


def kernel(
    groups,
    experts,
    span,
    capacity,
    out_pieces,
    w_pieces,
    res_in,
    gain_in,
    router_in,
    ids_in,
    wg_in,
    wu_in,
    wd_in,
    out_ref,
    res_ref,
    gain_ref,
    router_ref,
    ids_ref,
    tok,
    gates,
    act,
    rx,
    acc,
    picked,
    wg,
    wu,
    wd,
    in_sem,
    own_sem,
    land,
    tok_send,
    gate_recv,
    gate_send,
    ret_send,
    y_send,
    y_recv,
    x_send,
    x_recv,
    c_send,
    c_recv,
    cy_send,
    cy_recv,
    cx_send,
    cx_recv,
):
    rows, width = res_ref.shape
    grp = lax.axis_index("groups")
    pos = lax.axis_index("expert")
    exp = pos // span
    mem = pos % span
    last = experts - 1
    has_up = exp < last
    has_dn = exp > 0
    base = exp * span
    mem_y = (mem + 2) % 4
    mem_c = mem + 1 - 2 * (mem % 2)
    mem_yc = (mem_c + 2) % 4
    up = {"groups": grp, "expert": jnp.minimum(pos + span, experts * span - 1)}
    dn = {"groups": grp, "expert": jnp.maximum(pos - span, 0)}
    to_y = {"groups": grp, "expert": base + mem_y}
    to_c = {"groups": grp, "expert": base + mem_c}

    def other(i):
        return (grp + 1 + i) % groups

    barrier = pltpu.get_barrier_semaphore()

    def greet(device):
        pl.semaphore_signal(barrier, inc=1, device_id=device, device_id_type=MESH)

    greet(to_y)
    greet(to_c)
    for i in range(groups - 1):
        greet({"groups": other(i), "expert": pos})

    @pl.when(has_up)
    def _():
        greet(up)

    @pl.when(has_dn)
    def _():
        greet(dn)

    inputs = ((res_in, res_ref), (gain_in, gain_ref), (router_in, router_ref), (ids_in, ids_ref))
    loads = [pltpu.make_async_copy(*pair, in_sem.at[i]) for i, pair in enumerate(inputs)]
    for load in loads:
        load.start()

    mats = ((wg_in, wg), (wu_in, wu), (wd_in, wd))
    counts = (w_pieces, w_pieces, out_pieces)

    def piece(ref, mat, group, index):
        total = mats[mat][0].shape[mat // 2]
        size = total // groups // counts[mat]
        part = pl.ds(pl.multiple_of((index * groups + group) * size, size), size)
        return ref.at[:, part] if mat == 2 else ref.at[part]

    def number(mat, index):
        return sum(counts[:mat]) + index

    def remote(src, dst, send, recv, device):
        return pltpu.make_async_remote_copy(
            src_ref=src, dst_ref=dst, send_sem=send, recv_sem=recv, device_id=device, device_id_type=MESH
        )

    def y_copy(mat, index, landing):
        at = number(mat, index)
        ref = piece(mats[mat][1].at[mem_y if landing else mem], mat, grp, index)
        return remote(ref, ref, y_send.at[mat], y_recv.at[at], to_y)

    def x_copy(mat, index, i, landing):
        at = index if mat < 2 else w_pieces + index
        group = (grp + groups - 1 - i) % groups if landing else grp
        ref = piece(mats[mat][1].at[mem_y], mat, group, index)
        return remote(ref, ref, x_send.at[i, mat], x_recv.at[i, at], {"groups": other(i), "expert": pos})

    def landed(mat, index):
        return mat if mat < 2 else 2 + index

    def cy_copy(mat, index, landing):
        at = landed(mat, index)
        ref = piece(mats[mat][1].at[mem_yc if landing else mem_y], mat, grp, index)
        return remote(ref, ref, cy_send.at[mat], cy_recv.at[at], to_c)

    def cx_copy(mat, index, i, landing):
        at = landed(mat, index)
        group = (grp + groups - 1 - i) % groups
        ref = piece(mats[mat][1].at[mem_yc if landing else mem_y], mat, group, index)
        return remote(ref, ref, cx_send.at[i, mat], cx_recv.at[i, at], to_c)

    def all_pieces(mat, send, recv, device):
        ref = mats[mat][1].at[mem_y]
        part = pl.ds(0, mats[mat][0].shape[mat // 2] // groups)
        ref = ref.at[:, part] if mat == 2 else ref.at[part]
        return remote(ref, ref, send, recv, device)

    def c_copy(mat, landing):
        ref = mats[mat][1].at[mem_c if landing else mem]
        return remote(ref, ref, c_send.at[mat], c_recv.at[mat], to_c)

    def loop(count, body):
        def run(i, carry):
            body(i)
            return carry

        lax.fori_loop(0, count, run, 0)

    def start_pair(index):
        for mat in range(2):
            y_copy(mat, index, False).start()

    own_copies = [pltpu.make_async_copy(mats[i][0], mats[i][1].at[mem], own_sem.at[i]) for i in range(3)]
    for mat in range(3):
        own_copies[mat].start()

    step_rows = rows // TOK_PIECES
    tail = TOK_PIECES - HEAD
    ticks = (experts - 2) * TOK_PIECES
    behind = (exp, last - exp)
    onward = (has_up, has_dn)

    def tok_copy(block, index, way):
        ref = tok.at[block, pl.ds(pl.multiple_of(index * step_rows, step_rows), step_rows)]
        return remote(ref, ref, tok_send.at[way, block], land.at[block, index], (up, dn)[way])

    def gate_copy(block, way):
        ref = gates.at[block]
        return remote(ref, ref, gate_send.at[way, block], gate_recv.at[block], (up, dn)[way])

    def norm_rows(index):
        at = pl.ds(pl.multiple_of(index * step_rows, step_rows), step_rows)
        wide = res_ref[at, :].astype(jnp.float32)
        mean = jnp.mean(wide * wide, axis=1, keepdims=True)
        tok[exp, at, :] = (wide * lax.rsqrt(mean + norm_eps) * gain_ref[...].reshape(1, width)).astype(jnp.bfloat16)

    def first_rows(index):
        for way in range(2):
            early = jnp.logical_or(index < HEAD, behind[way] == 0)

            @pl.when(jnp.logical_and(onward[way], early))
            def _():
                tok_copy(exp, index, way).start()

    def gate_values():
        logits = lax.dot_general(
            router_ref[...], tok[exp], (((1,), (1,)), ((), ())), preferred_element_type=jnp.float32
        )
        affinity = jax.nn.sigmoid(logits)
        expert = lax.broadcasted_iota(jnp.int32, (experts, rows), 0)
        spread = jnp.zeros((experts, rows), jnp.float32)
        for k in range(ids_ref.shape[0]):
            spread = spread + jnp.where(expert == ids_ref[k : k + 1, :], affinity, 0.0)
        gates[exp] = route_scale * spread / jnp.sum(spread, axis=0, keepdims=True)

    peers = 1 + groups + has_up.astype(jnp.int32) + has_dn.astype(jnp.int32)
    pl.semaphore_wait(barrier, peers)
    for mat in range(2):
        own_copies[mat].wait()
    loop(w_pieces, start_pair)
    for load in loads:
        load.wait()

    def first_step(index):
        norm_rows(index)
        first_rows(index)

    loop(TOK_PIECES, first_step)
    own_copies[2].wait()
    loop(out_pieces, lambda index: y_copy(2, index, False).start())
    for mat in range(3):
        c_copy(mat, False).start()
    gate_values()
    for way in range(2):

        @pl.when(jnp.logical_and(onward[way], behind[way] == 0))
        def _():
            gate_copy(exp, way).start()

    def weight_tick(mat, index):
        y_copy(mat, index, True).wait_recv()
        for i in range(groups - 1):
            x_copy(mat, index, i, False).start()
        cy_copy(mat, index, False).start()

    def weight_late(index):
        for i in range(groups - 1):
            x_copy(2, index, i, True).wait_recv()
            cx_copy(2, index, i, False).start()

    def pair_late(index):
        both = wg.at[mem_y].at[pl.ds(0, 2 * (width // groups // w_pieces))]
        for i in range(groups - 1):
            device = {"groups": other(i), "expert": pos}
            remote(both, both, x_send.at[i, 0], x_recv.at[i, index], device).wait_recv()
            for mat in range(2):
                cx_copy(mat, index, i, False).start()

    def down_there(index):
        cy_copy(2, index, True).wait_recv()
        for i in range(groups - 1):
            cx_copy(2, index, i, True).wait_recv()

    def token_tick(step, way):
        tick = jnp.maximum(step, 0)
        count = behind[way]
        rest = jnp.maximum(tick - count * HEAD, 0)
        leading = tick < count * HEAD
        dist = jnp.where(leading, tick // HEAD + 1, count - rest // tail)
        dist = jnp.maximum(dist, 1)
        index = jnp.where(leading, tick % HEAD, HEAD + rest % tail)
        block = jnp.maximum(exp - dist, 0) if way == 0 else jnp.minimum(exp + dist, last)
        whole = index == TOK_PIECES - 1

        @pl.when(jnp.logical_and(step >= 0, tick < count * TOK_PIECES))
        def _():
            tok_copy(block, index, way).wait_recv()

            @pl.when(whole)
            def _():
                gate_copy(block, way).wait_recv()

            @pl.when(onward[way])
            def _():
                tok_copy(block, index, way).start()

                @pl.when(whole)
                def _():
                    gate_copy(block, way).start()

                @pl.when(tick == count * TOK_PIECES - 1)
                def _():
                    for own in range(HEAD, TOK_PIECES):
                        tok_copy(exp, own, way).start()
                    gate_copy(exp, way).start()

    def hidden_part(block, slot):
        rows_in = tok[block]
        gate_proj = jnp.dot(rows_in, wg[slot], preferred_element_type=jnp.float32)
        up_proj = jnp.dot(rows_in, wu[slot], preferred_element_type=jnp.float32)
        sublane = lax.broadcasted_iota(jnp.int32, (gates.shape[1], rows), 0)
        row = jnp.sum(jnp.where(sublane == exp, gates[block], 0.0), axis=0, keepdims=True)
        scale = jnp.broadcast_to(row, (LANES, rows)).T[:, :1]
        hidden = gate_proj / (1.0 + jnp.exp(-gate_proj)) * up_proj * scale
        act[slot, block] = hidden.astype(jnp.bfloat16)

    def whole_at(way, dist):
        count = behind[way]
        return count * HEAD + (count - dist + 1) * tail

    def found(tick, way):
        count = behind[way]
        over = tick + 1 - count * HEAD
        dist = count + 1 - over // tail
        there = jnp.logical_and(over > 0, over % tail == 0)
        return jnp.logical_and(there, jnp.logical_and(dist >= 1, dist <= count)), dist

    def first_tick(tick):
        @pl.when(tick < w_pieces)
        def _():
            weight_tick(0, tick)

        @pl.when(tick == w_pieces)
        def _():
            weight_tick(2, 0)

        token_tick(tick - 1, 0)
        token_tick(tick - 1, 1)

        @pl.when(tick < w_pieces)
        def _():
            weight_tick(1, tick)

        before = tick - LATE

        @pl.when(jnp.logical_and(before >= 0, before < w_pieces))
        def _():
            pair_late(jnp.maximum(before, 0))

        @pl.when(tick == OWN_TICK)
        def _():
            for mat in range(2):
                c_copy(mat, True).wait_recv()

        from_dn, dist_dn = found(tick - 1, 0)
        from_up, dist_up = found(tick - 1, 1)
        own = tick == OWN_TICK

        def job(i):
            side = i // 2
            slot = jnp.where(i % 2 == 0, mem, mem_c)
            block = jnp.where(side == 0, exp - dist_dn, jnp.where(side == 1, exp + dist_up, exp))
            valid = jnp.logical_or(
                jnp.logical_and(side == 0, from_dn),
                jnp.logical_or(jnp.logical_and(side == 1, from_up), jnp.logical_and(side == 2, own)),
            )

            @pl.when(valid)
            def _():
                hidden_part(jnp.clip(block, 0, last), slot)

        @pl.when(jnp.logical_or(own, jnp.logical_or(from_dn, from_up)))
        def _():
            loop(6, job)

    def packing(block, expert):
        sublane = lax.broadcasted_iota(jnp.int32, (gates.shape[1], rows), 0)
        row = jnp.sum(jnp.where(sublane == expert, gates[block], 0.0), axis=0, keepdims=True)
        taken = jnp.broadcast_to(jnp.where(row != 0.0, 1.0, 0.0), (capacity, rows))
        source = lax.broadcasted_iota(jnp.int32, (rows, rows), 0)
        dest = lax.broadcasted_iota(jnp.int32, (rows, rows), 1)
        earlier = jnp.where(source < dest, 1.0, 0.0).astype(jnp.bfloat16)
        rank = jnp.dot(taken.astype(jnp.bfloat16), earlier, preferred_element_type=jnp.float32)
        slot = lax.broadcasted_iota(jnp.int32, (capacity, rows), 0).astype(jnp.float32)
        return jnp.where(rank == slot, taken, 0.0).astype(jnp.bfloat16)

    at_end = jnp.logical_or(exp == 0, exp == last)

    end_way = jnp.where(exp == 0, 0, 1)

    def pick(block):
        picked[end_way, block] = packing(block, exp)

    def pack(block, slot):
        act[slot, block, pl.ds(0, capacity)] = jnp.dot(
            picked[end_way, block], act[slot, block], preferred_element_type=jnp.float32
        ).astype(jnp.bfloat16)

    def pick_far(i):
        block = jnp.where(exp == 0, last - i, i)
        pick(block)
        pack(block, mem)
        pack(block, mem_c)

    total = max(ticks, w_pieces) + 1
    loop(total, first_tick)
    rest = list(range(total - LATE, w_pieces))
    weight_tick(2, 1)

    @pl.when(at_end)
    def _():
        loop(last - 2, pick_far)

    for index in rest:
        pair_late(index)
    weight_tick(2, 2)

    def far_job(first, i):
        dist = last - i // 2
        side = i % 2
        valid = False
        for way in range(2):
            full = jnp.logical_and(dist <= behind[way], whole_at(way, dist) <= ticks)
            valid = jnp.logical_or(valid, jnp.logical_and(side == way, full))
        block = jnp.where(side == 0, exp - dist, exp + dist)

        @pl.when(valid)
        def _():
            slot = mem_y if first else mem_yc
            hidden_part(jnp.clip(block, 0, last), slot)

            @pl.when(at_end)
            def _():
                pack(jnp.clip(block, 0, last), slot)

    def far_first(i):
        far_job(True, i)

        @pl.when(i == 1)
        def _():
            weight_late(0)

    def far_second(i):
        far_job(False, i)
        order = i // 2

        @pl.when(jnp.logical_and(i % 2 == 1, order < RELAYS))
        def _():
            weight_tick(2, AHEAD + jnp.minimum(order, RELAYS - 1))

    loop(2 * last, far_first)
    for mat in range(2):
        all_pieces(mat, cy_send.at[mat], cy_recv.at[mat], to_c).wait_recv()
        for i in range(groups - 1):
            all_pieces(mat, cx_send.at[i, mat], cx_recv.at[i, mat], to_c).wait_recv()
    loop(2 * last, far_second)
    weight_late(1)
    sent_on = AHEAD + RELAYS
    c_copy(2, True).wait_recv()

    cols = width // out_pieces

    def columns(index):
        return pl.ds(pl.multiple_of(index * cols, cols), cols)

    def out_copy(block, index, way, landing, packed):
        part = columns(index)
        height = pl.ds(0, capacity if packed else rows)
        target = exp if landing else exp - 1
        into = jnp.where(jnp.logical_and(way == 1, block == target), experts, block)
        along = jnp.where(way == 0, jnp.minimum(pos + span, experts * span - 1), jnp.maximum(pos - span, 0))
        return remote(
            tok.at[block, height, part],
            rx.at[into, height, part],
            ret_send.at[block],
            land.at[into, index],
            {"groups": grp, "expert": along},
        )

    def share(block, at, height=rows):
        part = pl.ds(0, height)
        result = jnp.dot(act[0, block, part], wd[0, :, at], preferred_element_type=jnp.float32)
        for slot in range(1, span):
            result = result + jnp.dot(act[slot, block, part], wd[slot, :, at], preferred_element_type=jnp.float32)
        return result

    def unpacked(way, block, value):
        return lax.dot_general(
            picked[way, block], value, (((0,), (0,)), ((), ())), preferred_element_type=jnp.float32
        )

    def late_rows(block, dist):
        for index in range(HEAD, TOK_PIECES):

            @pl.when(jnp.logical_or(dist == 1, index >= TOK_PIECES - HEAD))
            def _():
                tok_copy(block, index, 0).wait_recv()

        gate_copy(block, 0).wait_recv()
        pick(block)

    def send_result(block, index, way, count):
        at = columns(index)

        @pl.when(count == 0)
        def _():
            tok[block, pl.ds(0, capacity), at] = share(block, at, capacity).astype(jnp.bfloat16)
            out_copy(block, index, way, False, True).start()

        @pl.when(jnp.logical_and(count > 0, index == 0))
        def _():
            rows_sent(block, 1 - way)

        @pl.when(count == 1)
        def _():
            @pl.when(index == 0)
            def _():
                picked[way, block] = packing(block, jnp.where(way == 0, exp - 1, exp + 1))

            out_copy(block, index, way, True, True).wait_recv()
            result = share(block, at) + unpacked(way, block, rx[block, pl.ds(0, capacity), at])
            tok[block, :, at] = result.astype(jnp.bfloat16)

        @pl.when(count > 1)
        def _():
            out_copy(block, index, way, True, False).wait_recv()
            result = share(block, at) + rx[block, :, at].astype(jnp.float32)
            tok[block, :, at] = result.astype(jnp.bfloat16)

        @pl.when(count > 0)
        def _():
            out_copy(block, index, way, False, False).start()

    def rows_sent(block, way):
        along = jnp.where(way == 0, up["expert"], dn["expert"])
        device = {"groups": grp, "expert": along}
        ref = tok.at[block]
        remote(ref, ref, tok_send.at[way, block], land.at[block, 0], device).wait_send()
        ref = gates.at[block]
        remote(ref, ref, gate_send.at[way, block], gate_recv.at[block], device).wait_send()

    def join(index, way, count):
        at = columns(index)
        slot = jnp.where(way == 0, exp, experts)

        @pl.when(count == 1)
        def _():
            @pl.when(index == 0)
            def _():
                picked[way, exp] = packing(exp, jnp.where(way == 0, exp - 1, exp + 1))

            out_copy(exp, index, way, True, True).wait_recv()
            acc[:, at] += unpacked(way, exp, rx[slot, pl.ds(0, capacity), at])

        @pl.when(count > 1)
        def _():
            out_copy(exp, index, way, True, False).wait_recv()
            acc[:, at] += rx[slot, :, at].astype(jnp.float32)

        out_ref[:, at] = acc[:, at].astype(jnp.bfloat16)

    period = out_pieces + SHIFT

    def after(far):
        return far // 2 * period + far % 2 * SHIFT + out_pieces

    def joins(count):
        far = last - count
        start = LAG * count + far // 2 * period + far % 2 * SHIFT + JOIN_LAG
        start = jnp.where(count == last, after(last - 1), start)
        start = jnp.where(count == 1, LAG + after(last - 2) - JOIN_TICKS, start)
        rate = jnp.where(count == 1, JOINS, jnp.where(count == last, 2, 1))
        return start, rate

    def until(count):
        start, rate = joins(count)
        send_end = LAG * count + after(jnp.maximum(last - count - 1, 0))
        join_end = start + (out_pieces + rate - 1) // jnp.maximum(rate, 1)
        return jnp.maximum(jnp.where(count < last, send_end, 0), jnp.where(count > 0, join_end, 0))

    own_start = jnp.where(at_end, 2 * (period // 2 + 1), OWN_START)

    def tick_job(tick):
        block, slot, due = exp, jnp.where(tick == own_start, mem_y, mem_yc), tick // 2 == own_start // 2
        for dist in (1, 2):
            first = (last - dist) // 2 * period + (last - dist) % 2 * SHIFT - SHIFT
            away = jnp.where(exp == 0, dist, last - dist)
            begins = jnp.logical_and(at_end, tick == first)

            @pl.when(begins)
            def _():
                late_rows(away, dist)

            turn = tick - first
            now = jnp.logical_and(at_end, jnp.logical_and(turn >= 0, turn < span))
            block, slot = jnp.where(now, away, block), jnp.where(now, (mem + turn) % span, slot)
            due = jnp.logical_or(due, now)

        @pl.when(due)
        def _():
            hidden_part(block, slot)

            @pl.when(block != exp)
            def _():
                pack(block, slot)

    def join_tick(tick, way):
        count = behind[way]
        start, rate = joins(count)

        def one(i):
            index = (tick - start) * rate + i

            @pl.when(jnp.logical_and(index >= 0, index < out_pieces))
            def _():
                join(jnp.clip(index, 0, out_pieces - 1), way, count)

        @pl.when(jnp.logical_and(count > 0, tick >= start))
        def _():
            loop(rate, one)

    def role(tick, i):
        way = i % 2
        second = i // 2
        count = jnp.where(way == 0, exp, last - exp)
        ahead = last - count
        time = tick - LAG * count
        clock = jnp.maximum(time, 0)
        pair = clock // period
        index = clock % period - SHIFT * second
        far = 2 * pair + second
        dist = ahead - far
        block = jnp.clip(jnp.where(way == 0, exp + dist, exp - dist), 0, last)
        there = jnp.logical_and(time >= 0, jnp.logical_and(index >= 0, index < out_pieces))
        index = jnp.clip(index, 0, out_pieces - 1)

        @pl.when(jnp.logical_and(there, dist > 0))
        def _():
            send_result(block, index, way, count)

    def second_tick(tick):
        @pl.when(tick < out_pieces)
        def _():
            down_there(jnp.minimum(tick, out_pieces - 1))

        loop(4, lambda i: role(tick, i))
        tick_job(tick)

        @pl.when(tick + sent_on < out_pieces)
        def _():
            weight_tick(2, jnp.minimum(tick + sent_on, out_pieces - 1))

        @pl.when(tick + 2 < out_pieces)
        def _():
            weight_late(jnp.minimum(tick + 2, out_pieces - 1))

        turn = tick - own_start - 1

        @pl.when(jnp.logical_and(turn >= 0, turn < out_pieces))
        def _():
            at = columns(jnp.clip(turn, 0, out_pieces - 1))
            acc[:, at] = res_ref[:, at].astype(jnp.float32) + share(exp, at)

        join_tick(tick, 0)
        join_tick(tick, 1)

    loop(jnp.maximum(until(behind[0]), until(behind[1])), second_tick)

    for way in range(2):

        @pl.when(onward[way])
        def _():
            rows_sent(exp, way)

    def results_sent(block):
        for way in range(2):
            passes = block > exp if way == 0 else block < exp
            for packed in (True, False):

                @pl.when(jnp.logical_and(passes, (behind[way] == 0) == packed))
                def _():
                    ref = tok.at[block, pl.ds(0, capacity if packed else rows)]
                    remote(ref, ref, ret_send.at[block], land.at[block, 0], (up, dn)[way]).wait_send()

    loop(experts, results_sent)
    for mat in range(3):
        c_copy(mat, False).wait_send()
        all_pieces(mat, y_send.at[mat], y_recv.at[mat], to_y).wait_send()
        all_pieces(mat, cy_send.at[mat], cy_recv.at[mat], to_c).wait_send()
        for i in range(groups - 1):
            device = {"groups": other(i), "expert": pos}
            all_pieces(mat, x_send.at[i, mat], x_recv.at[i, mat], device).wait_send()
            all_pieces(mat, cx_send.at[i, mat], cx_recv.at[i, mat], to_c).wait_send()


def shards(residual, norm_gain, router, w_gate, w_up, w_down, expert_ids):
    rows, width = residual.shape
    experts = router.shape[1]
    groups = lax.axis_size("groups")
    span = lax.axis_size("expert") // experts
    assert span == 4
    hid = w_gate.shape[1]
    capacity = 3 * rows * expert_ids.shape[1] // (2 * experts)
    capacity = min(rows, -(-capacity // 16) * 16)
    out_pieces = min(OUT_PIECES, width // (groups * LANES))
    w_pieces = W_PIECES
    while width // groups // w_pieces % 16:
        w_pieces //= 2
    vmem = pl.BlockSpec(memory_space=pltpu.VMEM)
    anywhere = pl.BlockSpec(memory_space=pl.ANY)
    dma = pltpu.SemaphoreType.DMA
    weight_copies = 2 * w_pieces + out_pieces
    return pl.pallas_call(
        functools.partial(kernel, groups, experts, span, capacity, out_pieces, w_pieces),
        out_shape=pltpu.VMEM((rows, width), jnp.bfloat16),
        in_specs=[anywhere] * 7,
        out_specs=vmem,
        scratch_shapes=[
            pltpu.VMEM((rows, width), residual.dtype),
            pltpu.VMEM((width,), norm_gain.dtype),
            pltpu.VMEM((experts, width), router.dtype),
            pltpu.VMEM(expert_ids.shape[::-1], expert_ids.dtype),
            pltpu.VMEM((experts, rows, width), jnp.bfloat16),
            pltpu.VMEM((experts, experts, rows), jnp.float32),
            pltpu.VMEM((span, experts, rows, hid), jnp.bfloat16),
            pltpu.VMEM((experts + 1, rows, width), jnp.bfloat16),
            pltpu.VMEM((rows, width), jnp.float32),
            pltpu.VMEM((2, experts, capacity, rows), jnp.bfloat16),
            pltpu.VMEM((span, width, hid), jnp.bfloat16),
            pltpu.VMEM((span, width, hid), jnp.bfloat16),
            pltpu.VMEM((span, hid, width), jnp.bfloat16),
            dma((4,)),
            dma((3,)),
            dma((experts + 1, max(TOK_PIECES, out_pieces))),
            dma((2, experts)),
            dma((experts,)),
            dma((2, experts)),
            dma((experts,)),
            dma((3,)),
            dma((weight_copies,)),
            dma((groups - 1, 3)),
            dma((groups - 1, w_pieces + out_pieces)),
            dma((3,)),
            dma((3,)),
            dma((3,)),
            dma((2 + out_pieces,)),
            dma((groups - 1, 3)),
            dma((groups - 1, 2 + out_pieces)),
        ],
        compiler_params=pltpu.CompilerParams(
            collective_id=0, has_side_effects=True, vmem_limit_bytes=67043328 - 2 * rows * width
        ),
    )(residual, norm_gain, router.T, expert_ids.T, w_gate, w_up, w_down)


def solution(mesh):
    in_specs = (
        P(("groups", "expert"), None),
        P(),
        P(),
        P(None, "expert"),
        P(None, "expert"),
        P("expert", None),
        P(("groups", "expert"), None),
    )
    out_specs = P(("groups", "expert"), None)
    return jax.shard_map(shards, mesh=mesh, in_specs=in_specs, out_specs=out_specs, check_vma=False)
```
